128 devices in a mesh: row: 8 (over x, z_lo), col: 16 (over z_hi, y, core).
Axes of the slice: x: 4, y: 4, z: 4 (z_hi: 2, z_lo: 2; z = z_hi * 2 + z_lo), core: 2. Of those that a mesh axis runs over, the one named last changes fastest.
Arguments:
- image: bfloat16 [128, 512, 768], P('row', 'col'), may hold values from -6 to 6
- conv_taps: float32 [9, 768], replicated, may hold values from -0.5 to 0.5
- w_query: bfloat16 [768, 768], replicated, may hold values from -0.21875 to 0.21875
- w_key: bfloat16 [768, 768], replicated, may hold values from -0.21875 to 0.21875
- w_value: bfloat16 [768, 768], replicated, may hold values from -0.21875 to 0.21875
- w_out: bfloat16 [768, 768], replicated, may hold values from -0.21875 to 0.21875
- grad_out: bfloat16 [128, 512, 768], P('row', 'col'), may hold values from -6 to 6
Outputs:
- grad_image: bfloat16 [128, 512, 768], P('row', 'col')
- grad_weights: float32 [768, 3072], P(None, 'col')
- grad_conv: float32 [9, 768], P(None, 'col')
The draws below stay inside these ranges and needn't reach their ends.
All inputs are finite; a program needn't handle non-finite values.
Results may differ from the reference program's by a relative error of at most 0.022.
Values may be sent and summed in bfloat16 or wider, within the bound.
No kernel may reach another device: no remote copies, remote signals or barrier semaphores. Data moves between devices by JAX's collectives and lax.ppermute only.
A program may use at most 128 MiB of HBM per device.

```python
import math
from functools import partial
import jax
import jax.numpy as jnp
from jax import lax

C = 768
HEADS = 12
HD = 64
POOL = 8
H = 128
W = 512
N_ROW = 8


def raised(drawn, own_key, source, target, blocks, factor):
    def block_of(axis_at):
        return (jnp.arange(drawn.shape[axis_at]) // (drawn.shape[axis_at] // blocks)).reshape((-1,) + (1,) * (drawn.ndim - 1 - axis_at))

    near = jax.random.permutation(own_key, blocks)[block_of(target)]
    second = (block_of(target) + blocks // 2) % blocks
    return jnp.where((block_of(source) == near) | (block_of(source) == second), factor * drawn, drawn)


def shard_levels(own_key, dims, cuts, smallest, largest):
    def one(dim, shards_of):
        steps = jax.random.uniform(jax.random.fold_in(jax.random.fold_in(own_key, 6), dim), (shards_of,), jnp.float32, smallest / len(cuts), largest / len(cuts))
        return jnp.repeat(jnp.exp(steps), dims[dim] // shards_of).reshape((-1,) + (1,) * (len(dims) - dim - 1))

    level = one(*cuts[0])
    for cut in cuts[1:]:
        level = level * one(*cut)
    return level


def noise(stream_key, shape, scale, reach, shards=(), kind=jnp.bfloat16):
    values = jax.random.normal(stream_key, shape, jnp.float32) * scale
    if len(shards) > 0:
        values = shard_levels(stream_key, shape, shards, -0.22, 0.18) * values
    return jnp.clip(values, min=-reach, max=reach).astype(kind)


def noise_with(key, shape, scale, reach, split, heavy, kind=jnp.bfloat16):
    values = scale * jax.random.normal(key, shape, jnp.float32)
    if split:
        values = values * shard_levels(key, shape, split, -0.22, 0.18)
    return jnp.clip(raised(values, jax.random.fold_in(key, 3), *heavy), -reach, reach).astype(kind)


def setup_inputs(seed: int = 0) -> dict:
    arg_keys = jax.random.split(jax.random.key(seed), 8)
    image = noise(arg_keys[0], (H, W, C), 1.0, 6.0, ((0, 8), (1, 16)))
    conv_taps = jnp.clip(jax.random.uniform(arg_keys[1], (9, C), jnp.float32, -0.5, 0.5), -0.5, 0.5)
    w_query = noise(arg_keys[2], (C, C), C ** -0.5, 0.21875)
    w_key = noise(arg_keys[3], (C, C), C ** -0.5, 0.21875)
    w_value = noise(arg_keys[4], (C, C), C ** -0.5, 0.21875)
    w_out = noise(arg_keys[5], (C, C), C ** -0.5, 0.21875)
    grad_out = noise_with(arg_keys[6], (H, W, C), 1.0, 6.0, ((0, 8), (1, 16)), (0, 2, 8, 2.0))
    return dict(image=image, conv_taps=conv_taps, w_query=w_query, w_key=w_key, w_value=w_value, w_out=w_out, grad_out=grad_out)


EPSILON = 1e-05

def contract_first(left, right):
    return lax.dot_general(left, right, (((0,), (0,)), ((), ())), preferred_element_type=jnp.float32)

def contract_last(left, right):
    return lax.dot_general(left, right, (((1,), (1,)), ((), ())), preferred_element_type=jnp.float32)

def exact_first(left, right):
    return lax.dot_general(left, right, (((0,), (0,)), ((), ())), precision=lax.Precision.HIGHEST, preferred_element_type=jnp.float32)

def exact_last(left, right):
    return lax.dot_general(left, right, (((1,), (1,)), ((), ())), precision=lax.Precision.HIGHEST, preferred_element_type=jnp.float32)

def stencil(padded, taps, height, width, flipped):
    total = jnp.zeros((height, width, padded.shape[2]), jnp.float32)
    for tap_row in range(3):
        for tap_col in range(3):
            if flipped:
                window = padded[2 - tap_row:2 - tap_row + height, 2 - tap_col:2 - tap_col + width]
            else:
                window = padded[tap_row:tap_row + height, tap_col:tap_col + width]
            total = total + taps[3 * tap_row + tap_col] * window.astype(jnp.float32)
    return total

def attend(carry, inputs, key_heads, value_heads):
    grad_key, grad_value = carry
    query_block, dout_block = inputs
    softmax_scale = HD ** (-0.5)
    query_heads = query_block.reshape(-1, HEADS, HD).astype(jnp.float32)
    dout_heads = dout_block.reshape(-1, HEADS, HD).astype(jnp.float32)
    key_float = key_heads.astype(jnp.float32)
    value_float = value_heads.astype(jnp.float32)
    scores = jnp.einsum('qhd,khd->hqk', query_heads, key_float) * softmax_scale
    expons = jnp.exp(scores)
    probabilities = expons / lax.optimization_barrier(jnp.sum(expons, axis=-1, keepdims=True))
    weights = probabilities.astype(jnp.bfloat16)
    attended = jnp.einsum('hqk,khd->qhd', weights.astype(jnp.float32), value_float).astype(jnp.bfloat16)
    grad_probs = jnp.einsum('qhd,khd->hqk', dout_heads, value_float)
    deltas = jnp.einsum('qhd,qhd->hq', dout_heads, attended.astype(jnp.float32))
    grad_scores = (probabilities * (grad_probs - deltas[:, :, None]) * softmax_scale).astype(jnp.bfloat16)
    grad_query = jnp.einsum('hqk,khd->qhd', grad_scores.astype(jnp.float32), key_float).astype(jnp.bfloat16)
    grad_key = grad_key + jnp.einsum('hqk,qhd->khd', grad_scores.astype(jnp.float32), query_heads)
    grad_value = grad_value + jnp.einsum('hqk,qhd->khd', weights.astype(jnp.float32), dout_heads)
    return ((grad_key, grad_value), (attended.reshape(query_block.shape), grad_query.reshape(query_block.shape)))

def reference(image, conv_taps, w_query, w_key, w_value, w_out, grad_out):
    height, width, channels = image.shape
    padded = jnp.pad(image, ((1, 1), (1, 1), (0, 0)))
    mixed = image.astype(jnp.float32) + stencil(padded, conv_taps, height, width, False)
    hidden = mixed.astype(jnp.bfloat16)
    flat_hidden = hidden.reshape(-1, channels)
    query = jnp.dot(flat_hidden, w_query, preferred_element_type=jnp.float32).astype(jnp.bfloat16)
    pooled = hidden.astype(jnp.float32).reshape(height // POOL, POOL, width // POOL, POOL, channels).mean(axis=(1, 3))
    centre = lax.optimization_barrier(jnp.mean(pooled, axis=-1, keepdims=True))
    spread = lax.optimization_barrier(jnp.mean(jnp.square(pooled - centre), axis=-1, keepdims=True))
    inverse = lax.rsqrt(spread + EPSILON)
    standard = (pooled - centre) * inverse
    normed = standard.astype(jnp.bfloat16)
    cells = normed.reshape(-1, channels)
    keys = jnp.dot(cells, w_key, preferred_element_type=jnp.float32).astype(jnp.bfloat16)
    values = jnp.dot(cells, w_value, preferred_element_type=jnp.float32).astype(jnp.bfloat16)
    flat_grad = grad_out.reshape(-1, channels)
    dout = contract_last(flat_grad, w_out).astype(jnp.bfloat16)
    row_queries = query.reshape(N_ROW, -1, channels)
    row_dout = dout.reshape(N_ROW, -1, channels)
    row_keys = keys.reshape(N_ROW, -1, HEADS, HD)
    row_values = values.reshape(N_ROW, -1, HEADS, HD)
    block_rows = math.gcd(row_queries.shape[1], 512)
    blocks = row_queries.shape[1] // block_rows

    def one_row(inputs):
        queries_row, dout_row, keys_row, values_row = inputs
        empty_grad = jnp.zeros(keys_row.shape, jnp.float32)
        carry, produced = lax.scan(partial(attend, key_heads=keys_row, value_heads=values_row), (empty_grad, empty_grad), (queries_row.reshape(blocks, block_rows, channels), dout_row.reshape(blocks, block_rows, channels)))
        return (carry[0], carry[1], produced[0].reshape(-1, channels), produced[1].reshape(-1, channels))
    grad_key, grad_value, attended, grad_query = lax.map(one_row, (row_queries, row_dout, row_keys, row_values))
    attended = attended.reshape(-1, channels)
    grad_query = grad_query.reshape(-1, channels)
    grad_key = grad_key.reshape(-1, channels)
    grad_value = grad_value.reshape(-1, channels)
    grad_wout = contract_first(attended, flat_grad)
    grad_wquery = contract_first(flat_hidden, grad_query)
    grad_hidden = contract_last(grad_query, w_query)
    cells_float = cells.astype(jnp.float32)
    grad_wkey = exact_first(cells_float, grad_key)
    grad_wvalue = exact_first(cells_float, grad_value)
    grad_normed = exact_last(grad_key, w_key.astype(jnp.float32)) + exact_last(grad_value, w_value.astype(jnp.float32))
    grad_normed = grad_normed.reshape(normed.shape)
    grad_pooled = (grad_normed - lax.optimization_barrier(jnp.mean(grad_normed, axis=-1, keepdims=True)) - standard * lax.optimization_barrier(jnp.mean(grad_normed * standard, axis=-1, keepdims=True))) * inverse
    pooled_rows, pooled_cols = (grad_pooled.shape[0], grad_pooled.shape[1])
    spread_back = jnp.broadcast_to((grad_pooled / (POOL * POOL))[:, None, :, None, :], (pooled_rows, POOL, pooled_cols, POOL, channels)).reshape(height, width, channels)
    grad_mixed = grad_out.astype(jnp.float32) + grad_hidden.reshape(height, width, channels) + spread_back
    grad_padded = jnp.pad(grad_mixed, ((1, 1), (1, 1), (0, 0)))
    grad_image = (grad_mixed + stencil(grad_padded, conv_taps, height, width, True)).astype(jnp.bfloat16)
    tap_list = []
    for tap_row in range(3):
        for tap_col in range(3):
            window = padded[tap_row:tap_row + height, tap_col:tap_col + width].astype(jnp.float32)
            tap_list.append(lax.optimization_barrier(jnp.sum(grad_mixed * window, axis=(0, 1))))
    grad_conv = jnp.stack(tap_list, axis=0)
    grad_weights = jnp.concatenate([grad_wquery, grad_wkey, grad_wvalue, grad_wout], axis=1)
    return (grad_image, grad_weights, grad_conv)
```

```python
from functools import partial
import math

import jax
import jax.numpy as jnp
from jax import lax
from jax.sharding import PartitionSpec as P

HEADS = 12
HD = 64
POOL = 8
EPSILON = 1e-05
BF = jnp.bfloat16
F32 = jnp.float32

FINAL = (0, 1, 2, 3, 12, 13, 14, 15)
PARTNER = (5, 4, 7, 6, 9, 8, 11, 10)
SLICE_AT = tuple((FINAL.index(j) if j in FINAL else PARTNER.index(j)) for j in range(16))
PAIRS = [(j, j ^ 1) for j in range(16)]


def holder(piece, core):
    return FINAL[piece] if FINAL[piece] % 2 == core else PARTNER[piece]


SUM_GROUPS = [[q * 16 + holder(s, c) for s in range(8) for q in range(8)] for c in range(2)]
PLACE_GROUPS = [[q * 16 + holder(s, c) for c in range(2) for q in range(8)] for s in range(8)]
BOTH = ("row", "col")


def with_halo(cells, sides, width):
    for axis, dim in sides:
        count = lax.axis_size(axis)
        ends = count - 1
        head = lax.slice_in_dim(cells, 0, width, axis=dim)
        tail = lax.slice_in_dim(cells, cells.shape[dim] - width, cells.shape[dim], axis=dim)
        cells = jnp.concatenate(
            [
                lax.ppermute(tail, axis, [(i, (i + 1) % count) for i in range(ends)]),
                cells,
                lax.ppermute(head, axis, [((i + 1) % count, i) for i in range(ends)]),
            ],
            axis=dim,
        )
    return cells


def copy_for_each(x, axis):
    peers = lax.axis_size(axis)
    return lax.all_to_all(jnp.broadcast_to(x[None], (peers, *x.shape)), axis, 0, 0, tiled=True)


def contract_first(left, right):
    return lax.dot_general(left, right, (((0,), (0,)), ((), ())), preferred_element_type=F32)


def contract_last(left, right):
    return lax.dot_general(left, right, (((1,), (1,)), ((), ())), preferred_element_type=F32)


def stencil(padded, taps, height, width, flipped):
    total = jnp.zeros((height, width, padded.shape[2]), F32)
    for tap_row in range(3):
        for tap_col in range(3):
            if flipped:
                window = padded[
                    2 - tap_row : 2 - tap_row + height, 2 - tap_col : 2 - tap_col + width
                ]
            else:
                window = padded[tap_row : tap_row + height, tap_col : tap_col + width]
            total = total + taps[3 * tap_row + tap_col] * window.astype(F32)
    return total


def attend(query, dout, keys, values):
    scale = HD ** (-0.5)
    q = query.reshape(-1, HEADS, HD)
    d = dout.reshape(-1, HEADS, HD)
    k = keys.reshape(-1, HEADS, HD)
    v = values.reshape(-1, HEADS, HD)
    scores = jnp.einsum("qhd,khd->hqk", q, k, preferred_element_type=F32) * scale
    expons = jnp.exp(scores)
    probs = expons / jnp.sum(expons, axis=-1, keepdims=True)
    weights = probs.astype(BF)
    attended = jnp.einsum("hqk,khd->qhd", weights, v, preferred_element_type=F32).astype(BF)
    grad_probs = jnp.einsum("qhd,khd->hqk", d, v, preferred_element_type=F32)
    deltas = jnp.einsum("qhd,qhd->hq", d, attended, preferred_element_type=F32)
    grad_scores = (probs * (grad_probs - deltas[:, :, None]) * scale).astype(BF)
    grad_query = jnp.einsum("hqk,khd->qhd", grad_scores, k, preferred_element_type=F32).astype(BF)
    grad_key = jnp.einsum("hqk,qhd->khd", grad_scores, q, preferred_element_type=F32)
    grad_value = jnp.einsum("hqk,qhd->khd", weights, d, preferred_element_type=F32)
    n = query.shape[1]
    return (
        attended.reshape(-1, n),
        grad_query.reshape(-1, n),
        grad_key.reshape(-1, n).astype(BF),
        grad_value.reshape(-1, n).astype(BF),
    )


def on_device(image, conv_taps, w_query, w_key, w_value, w_out, grad_out):
    height, width, channels = image.shape
    half = channels // 2
    at_row, at_col = lax.axis_index("row"), lax.axis_index("col")
    core = at_col % 2
    flat_grad = grad_out.reshape(-1, channels)
    padded = with_halo(image, (("row", 0), ("col", 1)), 1)
    dout = contract_last(flat_grad, w_out).astype(BF)
    hidden = (image.astype(F32) + stencil(padded, conv_taps, height, width, False)).astype(BF)
    flat_hidden = hidden.reshape(-1, channels)
    pooled = (
        hidden.astype(F32)
        .reshape(height // POOL, POOL, width // POOL, POOL, channels)
        .mean(axis=(1, 3))
        .reshape(-1, channels)
    )
    centre = jnp.mean(pooled, axis=-1, keepdims=True)
    spread = jnp.mean(jnp.square(pooled - centre), axis=-1, keepdims=True)
    inverse = lax.rsqrt(spread + EPSILON)
    standard = (pooled - centre) * inverse
    n_own = standard.shape[0]
    cells = copy_for_each(standard.astype(BF), "col").reshape(-1, channels)
    query = jnp.dot(flat_hidden, w_query, preferred_element_type=F32).astype(BF)
    keys = jnp.dot(cells, w_key, preferred_element_type=F32).astype(BF)
    values = jnp.dot(cells, w_value, preferred_element_type=F32).astype(BF)
    cells_half = lax.dynamic_slice_in_dim(cells, core * half, half, axis=1)
    all_cells = copy_for_each(cells_half, "row").reshape(-1, half)
    attended, grad_query, grad_key, grad_value = attend(query, dout, keys, values)
    terms = jnp.concatenate([grad_key, grad_value], axis=1).reshape(16, n_own, 2 * channels)
    terms = lax.all_to_all(terms, "col", 0, 0, tiled=True)
    def half_terms(which):
        h = lax.dynamic_slice_in_dim(flat_hidden, which * half, half, axis=1)
        a = lax.dynamic_slice_in_dim(attended, which * half, half, axis=1)
        return jnp.concatenate([contract_first(grad_query, h), contract_first(flat_grad, a)], axis=0)

    theirs = lax.ppermute(half_terms(1 - core).astype(BF), "col", PAIRS)
    chip = (half_terms(core) + theirs.astype(F32)).astype(BF)
    got = lax.all_to_all(
        chip.reshape(64, 24, half), BOTH, 0, 0, tiled=True, axis_index_groups=SUM_GROUPS
    )
    grad_hidden = contract_last(grad_query, w_query)
    early = grad_out.astype(F32) + grad_hidden.reshape(height, width, channels)
    sums = jnp.sum(terms.astype(F32), axis=0)
    sums_bf = sums.astype(BF)
    grad_normed = contract_last(sums_bf[:, :channels], w_key) + contract_last(
        sums_bf[:, channels:], w_value
    )
    grad_pooled = (
        grad_normed
        - jnp.mean(grad_normed, axis=-1, keepdims=True)
        - standard * jnp.mean(grad_normed * standard, axis=-1, keepdims=True)
    ) * inverse
    spread_back = jnp.broadcast_to(
        (grad_pooled / (POOL * POOL)).reshape(height // POOL, 1, width // POOL, 1, channels),
        (height // POOL, POOL, width // POOL, POOL, channels),
    ).reshape(height, width, channels)
    grad_mixed = early + spread_back
    tap_list = []
    for tap_row in range(3):
        for tap_col in range(3):
            window = padded[tap_row : tap_row + height, tap_col : tap_col + width]
            tap_list.append(jnp.sum(grad_mixed * window.astype(F32), axis=(0, 1)))
    tap_terms = jnp.stack(tap_list, axis=0).astype(BF)
    kv = jnp.transpose(sums_bf.reshape(n_own, 8, 8, 24), (2, 1, 0, 3))
    kv = jnp.concatenate([kv[:, PARTNER[SLICE_AT[j]] - 4][:, None] for j in range(16)], axis=1)
    taps = jnp.transpose(tap_terms.reshape(9, 16, 48), (1, 0, 2))
    last = jnp.pad(taps[:, 8:], ((0, 0), (0, 7), (0, 0)))
    taps = jnp.broadcast_to(jnp.concatenate([taps[:, :8], last], axis=2)[None], (8, 16, 8, 96))
    block = jnp.pad(jnp.concatenate([kv, taps], axis=3), ((0, 0), (0, 0), (0, 0), (0, 8)))
    blocks = lax.all_to_all(block.reshape(128, 8, 128), BOTH, 0, 0, tiled=True)
    kv_piece = contract_first(blocks.reshape(1024, 128), all_cells)[:24].astype(BF)
    tap_sums = jnp.sum(blocks.astype(F32), axis=0)
    grad_conv = jnp.concatenate([tap_sums[:, 24:72], tap_sums[:1, 72:120]], axis=0)
    piece = jnp.sum(got.astype(F32), axis=0).astype(BF)
    parity = (at_col % 2) ^ ((at_col >= 4) & (at_col < 12)).astype(at_col.dtype)
    first = jnp.where(parity == 0, piece, kv_piece)
    second = jnp.where(parity == 0, kv_piece, piece)
    placed = jnp.broadcast_to(jnp.stack([first, second])[:, None], (2, 8, 24, half))
    placed = lax.all_to_all(
        placed.reshape(16, 24, half), BOTH, 0, 0, tiled=True, axis_index_groups=PLACE_GROUPS
    )
    grad_weights = jnp.transpose(placed.reshape(2, 192, half), (0, 2, 1)).reshape(channels, 192)
    grad_padded = with_halo(grad_mixed.astype(BF), (("row", 0), ("col", 1)), 1)
    grad_image = (grad_mixed + stencil(grad_padded, conv_taps, height, width, True)).astype(BF)
    return (grad_image, grad_weights.astype(F32), grad_conv)


def solution(mesh):
    return jax.shard_map(
        on_device,
        mesh=mesh,
        in_specs=(P("row", "col", None), P(), P(), P(), P(), P(), P("row", "col", None)),
        out_specs=(P("row", "col", None), P(None, "col"), P(None, "col")),
        check_vma=False,
    )
```

```python
from functools import partial

import jax
import jax.numpy as jnp
from jax import lax
from jax.experimental import pallas as pl
from jax.experimental.pallas import tpu as pltpu
from jax.sharding import PartitionSpec as P

HEADS = 12
HD = 64
POOL = 8
EPSILON = 1e-05
BF = jnp.bfloat16
F32 = jnp.float32
LANES = 128

FINAL = (0, 1, 2, 3, 12, 13, 14, 15)
PARTNER = (5, 4, 7, 6, 9, 8, 11, 10)
SLICE_AT = tuple((FINAL.index(j) if j in FINAL else PARTNER.index(j)) for j in range(16))
PAIRS = [(j, j ^ 1) for j in range(16)]
BOTH = ("row", "col")


def holder(piece, core):
    return FINAL[piece] if FINAL[piece] % 2 == core else PARTNER[piece]


SUM_GROUPS = [[q * 16 + holder(s, c) for s in range(8) for q in range(8)] for c in range(2)]
PLACE_GROUPS = [[q * 16 + holder(s, c) for c in range(2) for q in range(8)] for s in range(8)]


def from_both_sides(first, last, axis):
    count = lax.axis_size(axis)
    before = lax.ppermute(last, axis, [(i, (i + 1) % count) for i in range(count)])
    after = lax.ppermute(first, axis, [((i + 1) % count, i) for i in range(count)])
    return before, after


def edges_of(tile, is_first, is_last):
    top, bottom = from_both_sides(tile[0], tile[-1], "row")
    up = jnp.where(is_first, 0, top).astype(BF)
    down = jnp.where(is_last, 0, bottom).astype(BF)
    first = jnp.concatenate([up[:1], tile[:, 0], down[:1]], axis=0)
    last = jnp.concatenate([up[-1:], tile[:, -1], down[-1:]], axis=0)
    left, right = from_both_sides(first, last, "col")
    return top, bottom, left, right


def copy_for_each(x, axis):
    peers = lax.axis_size(axis)
    return lax.all_to_all(jnp.broadcast_to(x[None], (peers, *x.shape)), axis, 0, 0, tiled=True)


def dot(left, right, dims):
    return lax.dot_general(left, right, ((dims[0], dims[1]), ((), ())), preferred_element_type=F32)


def contract_first(left, right):
    return dot(left, right, ((0,), (0,)))


def contract_last(left, right):
    return dot(left, right, ((1,), (1,)))


def put_sides(padded, flags, top, bottom, left, right):
    padded[0, 8:40, :] = top[...].astype(F32) * flags[0].astype(F32)
    padded[17, 8:40, :] = bottom[...].astype(F32) * flags[1].astype(F32)
    first = left[...].astype(F32) * flags[2].astype(F32)
    last = right[...].astype(F32) * flags[3].astype(F32)
    for row in range(18):
        padded[row, 7:8, :] = first[row : row + 1]
        padded[row, 40:41, :] = last[row : row + 1]


def mix_kernel(
    flags, image, top, bottom, left, right, taps, hidden, standard, inverse, normed, padded, pools
):
    step = pl.program_id(0)
    put_sides(padded, flags, top, bottom, left, right)
    padded[1:17, 8:40, :] = image[...].astype(F32)
    weights = taps[...]
    for cell_row in range(2):
        column = jnp.zeros((32, LANES), F32)
        for row in range(cell_row * POOL, (cell_row + 1) * POOL):
            total = padded[row + 1, 8:40, :]
            for a in range(3):
                for b in range(3):
                    tap = 3 * a + b
                    total = total + weights[tap : tap + 1] * padded[row + a, 7 + b : 39 + b, :]
            rounded = total.astype(BF)
            hidden[row * 32 : (row + 1) * 32, :] = rounded
            column = column + rounded.astype(F32)
        for cell in range(4):
            one = jnp.sum(column[cell * POOL : (cell + 1) * POOL], axis=0, keepdims=True)
            at = 4 * cell_row + cell
            pools[step, at : at + 1, :] = one * (1.0 / (POOL * POOL))

    @pl.when(step == pl.num_programs(0) - 1)
    def _():
        blocks = pools.shape[0]
        scale = 1.0 / (blocks * LANES)
        pooled = [pools[i] for i in range(blocks)]
        centre = sum(jnp.sum(x, axis=1, keepdims=True) for x in pooled) * scale
        moved = [x - centre for x in pooled]
        spread = sum(jnp.sum(x * x, axis=1, keepdims=True) for x in moved) * scale
        factor = lax.rsqrt(spread + EPSILON)
        inverse[...] = jnp.broadcast_to(factor, inverse.shape)
        for i in range(blocks):
            at = slice(i * LANES, (i + 1) * LANES)
            own = moved[i] * factor
            standard[:, at] = own
            normed[:, :, at] = jnp.broadcast_to(own.astype(BF)[None], (16, 8, LANES))


def side_specs():
    return [
        pl.BlockSpec((32, LANES), lambda i: (0, i)),
        pl.BlockSpec((32, LANES), lambda i: (0, i)),
        pl.BlockSpec((18, LANES), lambda i: (0, i)),
        pl.BlockSpec((18, LANES), lambda i: (0, i)),
    ]


SCALARS = pl.BlockSpec(memory_space=pltpu.SMEM)


def mix(flags, image, sides, taps):
    height, width, channels = image.shape
    blocks = channels // LANES
    return pl.pallas_call(
        mix_kernel,
        grid=(blocks,),
        in_specs=[
            SCALARS,
            pl.BlockSpec((height, width, LANES), lambda i: (0, 0, i)),
            *side_specs(),
            pl.BlockSpec((9, LANES), lambda i: (0, i)),
        ],
        out_specs=[
            pl.BlockSpec((height * width, LANES), lambda i: (0, i)),
            pl.BlockSpec((8, channels), lambda i: (0, 0)),
            pl.BlockSpec((8, LANES), lambda i: (0, 0)),
            pl.BlockSpec((16, 8, channels), lambda i: (0, 0, 0)),
        ],
        out_shape=[
            jax.ShapeDtypeStruct((height * width, channels), BF),
            jax.ShapeDtypeStruct((8, channels), F32),
            jax.ShapeDtypeStruct((8, LANES), F32),
            jax.ShapeDtypeStruct((16, 8, channels), BF),
        ],
        scratch_shapes=[pltpu.VMEM((18, 48, LANES), F32), pltpu.VMEM((blocks, 8, LANES), F32)],
        cost_estimate=pl.CostEstimate(flops=8_000_000, bytes_accessed=2_000_000, transcendentals=0),
        name="mix",
    )(flags, image, *sides, taps)


def attend_kernel(query, dout, cells, w_key, w_value, attended, grad_query, sums):
    low = lax.broadcasted_iota(jnp.int32, (128, LANES), 1) < HD
    all_cells = cells[...]
    zero = jnp.zeros((128, LANES), BF)

    def two_heads(weight):
        both = jnp.dot(all_cells, weight[...], preferred_element_type=F32).astype(BF)
        return jnp.concatenate([jnp.where(low, both, zero), jnp.where(low, zero, both)], axis=0)

    keys = two_heads(w_key) * jnp.asarray(HD**-0.5, BF)
    values = two_heads(w_value)
    q, d = query[...], dout[...]
    grads = contract_last(d, values)
    expons = jnp.exp(contract_last(q, keys))
    probs, scores = [], []
    for head in range(2):
        own = expons[:, head * 128 : (head + 1) * 128]
        prob = own / jnp.sum(own, axis=1, keepdims=True)
        grad = grads[:, head * 128 : (head + 1) * 128]
        delta = jnp.sum(prob * grad, axis=1, keepdims=True)
        probs.append(prob.astype(BF))
        scores.append((prob * (grad - delta)).astype(BF))
    weights = jnp.concatenate(probs, axis=1)
    grad_scores = jnp.concatenate(scores, axis=1)
    attended[...] = jnp.dot(weights, values, preferred_element_type=F32).astype(BF)
    grad_query[...] = jnp.dot(grad_scores, keys, preferred_element_type=F32).astype(BF)
    grad_keys = contract_first(grad_scores, q)
    grad_values = contract_first(weights, d)
    grad_keys = jnp.where(low, grad_keys[:128], grad_keys[128:]) * (HD**-0.5)
    grad_values = jnp.where(low, grad_values[:128], grad_values[128:])
    sums[:, 0] = grad_keys.astype(BF).reshape(16, 8, LANES)
    sums[:, 1] = grad_values.astype(BF).reshape(16, 8, LANES)


def attend(query, dout, cells, w_key, w_value):
    tokens, channels = query.shape
    blocks = channels // LANES
    by_pair = pl.BlockSpec((tokens, LANES), lambda i: (0, i))
    weight = pl.BlockSpec((channels, LANES), lambda i: (0, i))
    return pl.pallas_call(
        attend_kernel,
        grid=(blocks,),
        in_specs=[
            by_pair,
            by_pair,
            pl.BlockSpec((128, channels), lambda i: (0, 0)),
            weight,
            weight,
        ],
        out_specs=[by_pair, by_pair, pl.BlockSpec((16, 2, 8, LANES), lambda i: (0, 0, 0, i))],
        out_shape=[
            jax.ShapeDtypeStruct((tokens, channels), BF),
            jax.ShapeDtypeStruct((tokens, channels), BF),
            jax.ShapeDtypeStruct((16, 2, 8, channels), BF),
        ],
        cost_estimate=pl.CostEstimate(
            flops=3_000_000_000, bytes_accessed=6_000_000, transcendentals=800_000
        ),
        name="attend",
    )(query, dout, cells, w_key, w_value)


def taps_kernel(flags, image, top, bottom, left, right, early, terms, windows, padded, lines):
    put_sides(padded, flags, top, bottom, left, right)
    padded[1:17, 8:40, :] = image[...].astype(F32)
    totals = [jnp.zeros((8, LANES), F32) for _ in range(9)]
    for row in range(16):
        grad = early[row]
        for a in range(3):
            for b in range(3):
                part = grad * padded[row + a, 7 + b : 39 + b, :]
                totals[3 * a + b] = totals[3 * a + b] + (
                    (part[:8] + part[8:16]) + (part[16:24] + part[24:])
                )
    for tap in range(9):
        terms[tap : tap + 1, :] = jnp.sum(totals[tap], axis=0, keepdims=True)
    for cell_row in range(2):
        for a in range(3):
            at = cell_row * POOL + a
            line = padded[at]
            for row in range(at + 1, at + POOL):
                line = line + padded[row]
            lines[...] = line
            for b in range(3):
                for cell in range(4):
                    part = lines[7 + b + 8 * cell : 15 + b + 8 * cell, :]
                    place = 4 * cell_row + cell
                    windows[3 * a + b, place : place + 1, :] = jnp.sum(part, axis=0, keepdims=True)


def tap_terms(flags, image, sides, early):
    height, width, channels = image.shape
    block = pl.BlockSpec((height, width, LANES), lambda i: (0, 0, i))
    return pl.pallas_call(
        taps_kernel,
        grid=(channels // LANES,),
        in_specs=[SCALARS, block, *side_specs(), block],
        out_specs=[
            pl.BlockSpec((9, LANES), lambda i: (0, i)),
            pl.BlockSpec((9, 8, LANES), lambda i: (0, 0, i)),
        ],
        out_shape=[
            jax.ShapeDtypeStruct((9, channels), F32),
            jax.ShapeDtypeStruct((9, 8, channels), F32),
        ],
        scratch_shapes=[pltpu.VMEM((18, 48, LANES), F32), pltpu.VMEM((48, LANES), F32)],
        cost_estimate=pl.CostEstimate(flops=8_000_000, bytes_accessed=3_000_000, transcendentals=0),
        name="tap_terms",
    )(flags, image, *sides, early)


def window_of(x, start):
    base = min(start // LANES * LANES, x.shape[1] - 2 * LANES)
    if start == base:
        return x[:, base : base + LANES]
    return pltpu.roll(x[:, base : base + 2 * LANES], base - start + 2 * LANES, 1)[:, :LANES]


def cells_kernel(terms, w_key, w_value, standard, inverse, early, windows, grad_pooled, blocks):
    received = jnp.sum(terms[...].astype(F32), axis=0)
    keys, values = received[0], received[1]
    grad = contract_last(keys.astype(BF), w_key[...]) + contract_last(values.astype(BF), w_value[...])
    own = standard[...]
    scale = 1.0 / own.shape[1]
    centre = jnp.sum(grad, axis=1, keepdims=True) * scale
    along = jnp.sum(grad * own, axis=1, keepdims=True) * scale
    pooled = (grad - centre - own * along) * (inverse[:, :1] * (1.0 / (POOL * POOL)))
    grad_pooled[...] = pooled
    conv = [
        early[t : t + 1, :] + jnp.sum(pooled * windows[t], axis=0, keepdims=True) for t in range(9)
    ]
    first, last = jnp.concatenate(conv[:8], axis=0), jnp.broadcast_to(conv[8], (8, own.shape[1]))
    lane = lax.broadcasted_iota(jnp.int32, (8, LANES), 1)
    both = jnp.concatenate([keys, values], axis=1)
    width = own.shape[1] // 16
    pieces = {}
    for j in range(16):
        part = PARTNER[SLICE_AT[j]] - 4
        taps = pltpu.roll(window_of(first, width * j), 24, 1)
        tail = pltpu.roll(window_of(last, width * j), 72, 1)
        rest = jnp.where(lane < 72, taps, tail)
        for q in range(8):
            if (part, q) not in pieces:
                pieces[part, q] = window_of(both, 192 * part + 24 * q)
            blocks[16 * q + j] = jnp.where(lane < 24, pieces[part, q], rest).astype(BF)


def at_cells(terms, w_key, w_value, standard, inverse, early, windows):
    channels = standard.shape[1]
    return pl.pallas_call(
        cells_kernel,
        out_shape=[
            jax.ShapeDtypeStruct((8, channels), F32),
            jax.ShapeDtypeStruct((128, 8, LANES), BF),
        ],
        cost_estimate=pl.CostEstimate(flops=30_000_000, bytes_accessed=3_500_000, transcendentals=0),
        name="at_cells",
    )(terms, w_key, w_value, standard, inverse, early, windows)


def pieces_kernel(flags, got, blocks, cells, placed, conv):
    piece = jnp.sum(got[...].astype(F32), axis=0).astype(BF)
    received = blocks[...]
    conv[...] = jnp.sum(received.astype(F32), axis=0)
    cell_piece = contract_first(received.reshape(1024, LANES), cells[...])[:24].astype(BF)
    odd = flags[4] == 1
    first = jnp.where(odd, cell_piece, piece)
    second = jnp.where(odd, piece, cell_piece)
    for q in range(8):
        placed[q] = first
        placed[8 + q] = second


def pieces(flags, got, blocks, cells):
    half = cells.shape[1]
    vmem = pl.BlockSpec(memory_space=pltpu.VMEM)
    return pl.pallas_call(
        pieces_kernel,
        in_specs=[SCALARS, vmem, vmem, vmem],
        out_shape=[
            jax.ShapeDtypeStruct((16, 24, half), BF),
            jax.ShapeDtypeStruct((8, LANES), F32),
        ],
        cost_estimate=pl.CostEstimate(flops=100_000_000, bytes_accessed=2_500_000, transcendentals=0),
        name="pieces",
    )(flags, got, blocks, cells)


def unmix_kernel(flags, early, pooled, top, bottom, left, right, taps, image, padded):
    put_sides(padded, flags, top, bottom, left, right)
    for row in range(16):
        for cell in range(4):
            place = 4 * (row // POOL) + cell
            at = slice(8 * cell, 8 * cell + 8)
            padded[row + 1, 8 + 8 * cell : 16 + 8 * cell, :] = (
                early[row, at, :] + pooled[place : place + 1, :]
            )
    weights = taps[...]
    for row in range(16):
        total = padded[row + 1, 8:40, :]
        for a in range(3):
            for b in range(3):
                tap = 3 * a + b
                total = total + weights[tap : tap + 1] * padded[row + 2 - a, 9 - b : 41 - b, :]
        image[row] = total.astype(BF)


def unmix(flags, early, pooled, sides, taps):
    height, width, channels = early.shape
    block = pl.BlockSpec((height, width, LANES), lambda i: (0, 0, i))
    return pl.pallas_call(
        unmix_kernel,
        grid=(channels // LANES,),
        in_specs=[
            SCALARS,
            block,
            pl.BlockSpec((8, LANES), lambda i: (0, i)),
            *side_specs(),
            pl.BlockSpec((9, LANES), lambda i: (0, i)),
        ],
        out_specs=block,
        out_shape=jax.ShapeDtypeStruct((height, width, channels), BF),
        scratch_shapes=[pltpu.VMEM((18, 48, LANES), F32)],
        cost_estimate=pl.CostEstimate(flops=8_000_000, bytes_accessed=3_000_000, transcendentals=0),
        name="unmix",
    )(flags, early, pooled, *sides, taps)


def on_device(image, conv_taps, w_query, w_key, w_value, w_out, grad_out):
    height, width, channels = image.shape
    half = channels // 2
    at_row, at_col = lax.axis_index("row"), lax.axis_index("col")
    core = at_col % 2
    is_first, is_last = at_row == 0, at_row == lax.axis_size("row") - 1
    turned = (core == 1) ^ ((at_col >= 4) & (at_col < 12))
    flags = jnp.stack(
        [
            ~is_first,
            ~is_last,
            at_col > 0,
            at_col < lax.axis_size("col") - 1,
            turned,
        ]
    ).astype(jnp.int32)
    flat_grad = grad_out.reshape(-1, channels)
    sides = edges_of(image, is_first, is_last)
    dout = contract_last(flat_grad, w_out).astype(BF)
    hidden, standard, inverse, normed = mix(flags, image, sides, conv_taps)
    cells = lax.all_to_all(normed, "col", 0, 0, tiled=True).reshape(-1, channels)
    query = jnp.dot(hidden, w_query, preferred_element_type=F32).astype(BF)
    cells_half = lax.dynamic_slice_in_dim(cells, core * half, half, axis=1)
    all_cells = copy_for_each(cells_half, "row").reshape(-1, half)
    attended, grad_query, sums = attend(query, dout, cells, w_key, w_value)
    terms = lax.all_to_all(sums, "col", 0, 0, tiled=True)

    def half_terms(which):
        h = lax.dynamic_slice_in_dim(hidden, which * half, half, axis=1)
        a = lax.dynamic_slice_in_dim(attended, which * half, half, axis=1)
        return jnp.concatenate([contract_first(grad_query, h), contract_first(flat_grad, a)], axis=0)

    theirs = lax.ppermute(half_terms(1 - core).astype(BF), "col", PAIRS)
    chip = (half_terms(core) + theirs.astype(F32)).astype(BF)
    got = lax.all_to_all(
        chip.reshape(64, 24, half), BOTH, 0, 0, tiled=True, axis_index_groups=SUM_GROUPS
    )
    grad_hidden = contract_last(grad_query, w_query)
    early = (flat_grad.astype(F32) + grad_hidden).reshape(height, width, channels)
    early_terms, windows = tap_terms(flags, image, sides, early)
    pooled, block = at_cells(terms, w_key, w_value, standard, inverse, early_terms, windows)
    blocks = lax.all_to_all(block, BOTH, 0, 0, tiled=True)
    rows = jnp.repeat(pooled, POOL, axis=0).reshape(2, width, channels)
    up = jnp.concatenate([pooled[0:1], pooled[4:5]], axis=0)
    down = jnp.concatenate([pooled[3:4], pooled[7:8]], axis=0)
    top, bottom = from_both_sides(
        (early[0] + rows[0]).astype(BF), (early[-1] + rows[1]).astype(BF), "row"
    )
    first = (early[:, 0] + jnp.repeat(up, POOL, axis=0)).astype(BF)
    last = (early[:, -1] + jnp.repeat(down, POOL, axis=0)).astype(BF)
    over = jnp.where(is_first, 0, top).astype(BF)
    under = jnp.where(is_last, 0, bottom).astype(BF)
    left, right = from_both_sides(
        jnp.concatenate([over[:1], first, under[:1]], axis=0),
        jnp.concatenate([over[-1:], last, under[-1:]], axis=0),
        "col",
    )
    grad_image = unmix(flags, early, pooled, (top, bottom, left, right), conv_taps)
    placed, conv = pieces(flags, got, blocks, all_cells)
    placed = lax.all_to_all(
        placed, BOTH, 0, 0, tiled=True, axis_index_groups=PLACE_GROUPS
    )
    grad_weights = jnp.transpose(placed.reshape(2, 192, half), (0, 2, 1)).reshape(channels, 192)
    grad_conv = jnp.concatenate([conv[:, 24:72], conv[:1, 72:120]], axis=0)
    return (grad_image, grad_weights.astype(F32), grad_conv)


def solution(mesh):
    return jax.shard_map(
        on_device,
        mesh=mesh,
        in_specs=(P("row", "col", None), P(), P(), P(), P(), P(), P("row", "col", None)),
        out_specs=(P("row", "col", None), P(None, "col"), P(None, "col")),
        check_vma=False,
    )
```

```python
import jax
import jax.numpy as jnp
from jax import lax
from jax.experimental import pallas as pl
from jax.experimental.pallas import tpu as pltpu
from jax.sharding import PartitionSpec as P

HD = 64
POOL = 8
EPSILON = 1e-05
BF = jnp.bfloat16
F32 = jnp.float32
LANES = 128

FINAL = (0, 1, 2, 3, 12, 13, 14, 15)
PARTNER = (5, 4, 7, 6, 9, 8, 11, 10)
SLICE_AT = tuple((FINAL.index(j) if j in FINAL else PARTNER.index(j)) for j in range(16))
PAIRS = [(j, j ^ 1) for j in range(16)]
BOTH = ("row", "col")


def holder(piece, core):
    return FINAL[piece] if FINAL[piece] % 2 == core else PARTNER[piece]


SUM_GROUPS = [[q * 16 + holder(s, c) for s in range(8) for q in range(8)] for c in range(2)]
PLACE_GROUPS = [[q * 16 + holder(s, c) for c in range(2) for q in range(8)] for s in range(8)]


def from_both_sides(first, last, axis):
    count = lax.axis_size(axis)
    before = lax.ppermute(last, axis, [(i, (i + 1) % count) for i in range(count)])
    after = lax.ppermute(first, axis, [((i + 1) % count, i) for i in range(count)])
    return before, after


def edges_of(tile, is_first, is_last):
    top, bottom = from_both_sides(tile[0], tile[-1], "row")
    up = jnp.where(is_first, 0, top).astype(BF)
    down = jnp.where(is_last, 0, bottom).astype(BF)
    first = jnp.concatenate([up[:1], tile[:, 0], down[:1]], axis=0)
    last = jnp.concatenate([up[-1:], tile[:, -1], down[-1:]], axis=0)
    left, right = from_both_sides(first, last, "col")
    return top, bottom, left, right


def dot(left, right, dims):
    return lax.dot_general(left, right, ((dims[0], dims[1]), ((), ())), preferred_element_type=F32)


def contract_first(left, right):
    return dot(left, right, ((0,), (0,)))


def contract_last(left, right):
    return dot(left, right, ((1,), (1,)))


def put_sides(padded, flags, top, bottom, left, right):
    padded[0, 8:40, :] = top[...].astype(F32) * flags[0].astype(F32)
    padded[17, 8:40, :] = bottom[...].astype(F32) * flags[1].astype(F32)
    first = left[...].astype(F32) * flags[2].astype(F32)
    last = right[...].astype(F32) * flags[3].astype(F32)
    for row in range(18):
        padded[row, 7:8, :] = first[row : row + 1]
        padded[row, 40:41, :] = last[row : row + 1]


def mix_kernel(
    flags, image, top, bottom, left, right, taps, hidden, standard, inverse, normed, padded, pools
):
    step = pl.program_id(0)
    put_sides(padded, flags, top, bottom, left, right)
    padded[1:17, 8:40, :] = image[...].astype(F32)
    weights = taps[...]
    for cell_row in range(2):
        column = jnp.zeros((32, LANES), F32)
        for row in range(cell_row * POOL, (cell_row + 1) * POOL):
            total = padded[row + 1, 8:40, :]
            for a in range(3):
                for b in range(3):
                    tap = 3 * a + b
                    total = total + weights[tap : tap + 1] * padded[row + a, 7 + b : 39 + b, :]
            rounded = total.astype(BF)
            hidden[row * 32 : (row + 1) * 32, :] = rounded
            column = column + rounded.astype(F32)
        for cell in range(4):
            one = jnp.sum(column[cell * POOL : (cell + 1) * POOL], axis=0, keepdims=True)
            at = 4 * cell_row + cell
            pools[step, at : at + 1, :] = one * (1.0 / (POOL * POOL))

    @pl.when(step == pl.num_programs(0) - 1)
    def _():
        blocks = pools.shape[0]
        scale = 1.0 / (blocks * LANES)
        pooled = [pools[i] for i in range(blocks)]
        centre = sum(jnp.sum(x, axis=1, keepdims=True) for x in pooled) * scale
        moved = [x - centre for x in pooled]
        spread = sum(jnp.sum(x * x, axis=1, keepdims=True) for x in moved) * scale
        factor = lax.rsqrt(spread + EPSILON)
        inverse[...] = jnp.broadcast_to(factor, inverse.shape)
        for i in range(blocks):
            at = slice(i * LANES, (i + 1) * LANES)
            own = moved[i] * factor
            standard[:, at] = own
            normed[:, :, at] = jnp.broadcast_to(own.astype(BF)[None], (16, 8, LANES))


def side_specs():
    return [
        pl.BlockSpec((32, LANES), lambda i: (0, i)),
        pl.BlockSpec((32, LANES), lambda i: (0, i)),
        pl.BlockSpec((18, LANES), lambda i: (0, i)),
        pl.BlockSpec((18, LANES), lambda i: (0, i)),
    ]


SCALARS = pl.BlockSpec(memory_space=pltpu.SMEM)


def mix(flags, image, sides, taps):
    height, width, channels = image.shape
    blocks = channels // LANES
    return pl.pallas_call(
        mix_kernel,
        grid=(blocks,),
        in_specs=[
            SCALARS,
            pl.BlockSpec((height, width, LANES), lambda i: (0, 0, i)),
            *side_specs(),
            pl.BlockSpec((9, LANES), lambda i: (0, i)),
        ],
        out_specs=[
            pl.BlockSpec((height * width, LANES), lambda i: (0, i)),
            pl.BlockSpec((8, channels), lambda i: (0, 0)),
            pl.BlockSpec((8, LANES), lambda i: (0, 0)),
            pl.BlockSpec((16, 8, channels), lambda i: (0, 0, 0)),
        ],
        out_shape=[
            jax.ShapeDtypeStruct((height * width, channels), BF),
            jax.ShapeDtypeStruct((8, channels), F32),
            jax.ShapeDtypeStruct((8, LANES), F32),
            jax.ShapeDtypeStruct((16, 8, channels), BF),
        ],
        scratch_shapes=[pltpu.VMEM((18, 48, LANES), F32), pltpu.VMEM((blocks, 8, LANES), F32)],
        cost_estimate=pl.CostEstimate(flops=8_000_000, bytes_accessed=2_000_000, transcendentals=0),
        name="mix",
    )(flags, image, *sides, taps)


def attend_kernel(
    flags, query, dout, cells, w_key, w_value, attended, grad_query, kept, sent
):
    low = lax.broadcasted_iota(jnp.int32, (128, LANES), 1) < HD
    all_cells = cells[...]
    zero = jnp.zeros((128, LANES), BF)

    def two_heads(weight):
        both = jnp.dot(all_cells, weight[...], preferred_element_type=F32).astype(BF)
        return jnp.concatenate([jnp.where(low, both, zero), jnp.where(low, zero, both)], axis=0)

    keys = two_heads(w_key) * jnp.asarray(HD**-0.5, BF)
    values = two_heads(w_value)
    q, d = query[...], dout[...]
    grads = contract_last(d, values)
    expons = jnp.exp(contract_last(q, keys))
    probs, scores = [], []
    for head in range(2):
        own = expons[:, head * 128 : (head + 1) * 128]
        prob = own / jnp.sum(own, axis=1, keepdims=True)
        grad = grads[:, head * 128 : (head + 1) * 128]
        delta = jnp.sum(prob * grad, axis=1, keepdims=True)
        probs.append(prob.astype(BF))
        scores.append((prob * (grad - delta)).astype(BF))
    weights = jnp.concatenate(probs, axis=1)
    grad_scores = jnp.concatenate(scores, axis=1)
    attended[...] = jnp.dot(weights, values, preferred_element_type=F32).astype(BF)
    grad_query[...] = jnp.dot(grad_scores, keys, preferred_element_type=F32).astype(BF)
    grad_keys = contract_first(grad_scores, q)
    grad_values = contract_first(weights, d)
    grad_keys = jnp.where(low, grad_keys[:128], grad_keys[128:]) * (HD**-0.5)
    grad_values = jnp.where(low, grad_values[:128], grad_values[128:])
    odd = flags[5] == 1
    for i, grad in enumerate((grad_keys, grad_values)):
        grad = grad.reshape(8, 2, 8, LANES)
        kept[:, i] = jnp.where(odd, grad[:, 1], grad[:, 0])
        sent[:, i] = jnp.where(odd, grad[:, 0], grad[:, 1]).astype(BF)


def attend(flags, query, dout, cells, w_key, w_value):
    tokens, channels = query.shape
    blocks = channels // LANES
    by_pair = pl.BlockSpec((tokens, LANES), lambda i: (0, i))
    weight = pl.BlockSpec((channels, LANES), lambda i: (0, i))
    sums = pl.BlockSpec((8, 2, 8, LANES), lambda i: (0, 0, 0, i))
    return pl.pallas_call(
        attend_kernel,
        grid=(blocks,),
        in_specs=[
            SCALARS,
            by_pair,
            by_pair,
            pl.BlockSpec((128, channels), lambda i: (0, 0)),
            weight,
            weight,
        ],
        out_specs=[by_pair, by_pair, sums, sums],
        out_shape=[
            jax.ShapeDtypeStruct((tokens, channels), BF),
            jax.ShapeDtypeStruct((tokens, channels), BF),
            jax.ShapeDtypeStruct((8, 2, 8, channels), F32),
            jax.ShapeDtypeStruct((8, 2, 8, channels), BF),
        ],
        cost_estimate=pl.CostEstimate(
            flops=3_000_000_000, bytes_accessed=6_000_000, transcendentals=800_000
        ),
        name="attend",
    )(flags, query, dout, cells, w_key, w_value)


def weights_kernel(which, grad_query, flat_grad, hidden, attended, *rest):
    terms = rest[-1]
    step = pl.program_id(0)

    def put(value):
        if len(rest) == 2:
            value = value + rest[0][...].astype(F32)
        terms[...] = value.astype(BF)

    @pl.when(step < 2)
    def _():
        put(contract_first(grad_query[...], hidden[...]))

    @pl.when(step >= 2)
    def _():
        put(contract_first(flat_grad[...], attended[...]))


def weight_terms(which, grad_query, flat_grad, hidden, attended, others=None):
    tokens, channels = hidden.shape
    half = channels // 2
    out = pl.BlockSpec((half, half), lambda i, w: (i, 0))
    operands = [grad_query, flat_grad, hidden, attended] + ([] if others is None else [others])
    return pl.pallas_call(
        weights_kernel,
        grid_spec=pltpu.PrefetchScalarGridSpec(
            num_scalar_prefetch=1,
            grid=(4,),
            in_specs=[
                pl.BlockSpec((tokens, half), lambda i, w: (0, jnp.minimum(i, 1))),
                pl.BlockSpec((tokens, half), lambda i, w: (0, jnp.maximum(i - 2, 0))),
                pl.BlockSpec((tokens, half), lambda i, w: (0, w[0])),
                pl.BlockSpec((tokens, half), lambda i, w: (0, w[0])),
            ]
            + ([] if others is None else [out]),
            out_specs=out,
        ),
        out_shape=jax.ShapeDtypeStruct((2 * channels, half), BF),
        cost_estimate=pl.CostEstimate(
            flops=600_000_000, bytes_accessed=4_000_000, transcendentals=0
        ),
        name="weight_terms",
    )(which, *operands)


def taps_kernel(flags, image, top, bottom, left, right, early, terms, windows, padded, lines):
    put_sides(padded, flags, top, bottom, left, right)
    padded[1:17, 8:40, :] = image[...].astype(F32)
    totals = [jnp.zeros((8, LANES), F32) for _ in range(9)]
    for row in range(16):
        grad = early[row]
        for a in range(3):
            for b in range(3):
                part = grad * padded[row + a, 7 + b : 39 + b, :]
                totals[3 * a + b] = totals[3 * a + b] + (
                    (part[:8] + part[8:16]) + (part[16:24] + part[24:])
                )
    for tap in range(9):
        terms[tap : tap + 1, :] = jnp.sum(totals[tap], axis=0, keepdims=True)
    for cell_row in range(2):
        for a in range(3):
            at = cell_row * POOL + a
            line = padded[at]
            for row in range(at + 1, at + POOL):
                line = line + padded[row]
            lines[...] = line
            for b in range(3):
                for cell in range(4):
                    part = lines[7 + b + 8 * cell : 15 + b + 8 * cell, :]
                    place = 4 * cell_row + cell
                    windows[3 * a + b, place : place + 1, :] = jnp.sum(part, axis=0, keepdims=True)


def tap_terms(flags, image, sides, early):
    height, width, channels = image.shape
    block = pl.BlockSpec((height, width, LANES), lambda i: (0, 0, i))
    return pl.pallas_call(
        taps_kernel,
        grid=(channels // LANES,),
        in_specs=[SCALARS, block, *side_specs(), block],
        out_specs=[
            pl.BlockSpec((9, LANES), lambda i: (0, i)),
            pl.BlockSpec((9, 8, LANES), lambda i: (0, 0, i)),
        ],
        out_shape=[
            jax.ShapeDtypeStruct((9, channels), F32),
            jax.ShapeDtypeStruct((9, 8, channels), F32),
        ],
        scratch_shapes=[pltpu.VMEM((18, 48, LANES), F32), pltpu.VMEM((48, LANES), F32)],
        cost_estimate=pl.CostEstimate(flops=8_000_000, bytes_accessed=3_000_000, transcendentals=0),
        name="tap_terms",
    )(flags, image, *sides, early)


def window_of(x, start):
    base = min(start // LANES * LANES, x.shape[1] - 2 * LANES)
    if start == base:
        return x[:, base : base + LANES]
    return pltpu.roll(x[:, base : base + 2 * LANES], base - start + 2 * LANES, 1)[:, :LANES]


def cells_kernel(kept, terms, w_key, w_value, standard, inverse, early, windows, grad_pooled, blocks):
    received = kept[...] + terms[...].astype(F32)
    keys, values = received[0], received[1]
    grad = contract_last(keys.astype(BF), w_key[...]) + contract_last(values.astype(BF), w_value[...])
    own = standard[...]
    scale = 1.0 / own.shape[1]
    centre = jnp.sum(grad, axis=1, keepdims=True) * scale
    along = jnp.sum(grad * own, axis=1, keepdims=True) * scale
    pooled = (grad - centre - own * along) * (inverse[:, :1] * (1.0 / (POOL * POOL)))
    grad_pooled[...] = pooled
    conv = [
        early[t : t + 1, :] + jnp.sum(pooled * windows[t], axis=0, keepdims=True) for t in range(9)
    ]
    first, last = jnp.concatenate(conv[:8], axis=0), jnp.broadcast_to(conv[8], (8, own.shape[1]))
    lane = lax.broadcasted_iota(jnp.int32, (8, LANES), 1)
    both = jnp.concatenate([keys, values], axis=1)
    width = own.shape[1] // 16
    pieces = {}
    for j in range(16):
        part = PARTNER[SLICE_AT[j]] - 4
        taps = pltpu.roll(window_of(first, width * j), 24, 1)
        tail = pltpu.roll(window_of(last, width * j), 72, 1)
        rest = jnp.where(lane < 72, taps, tail)
        for q in range(8):
            if (part, q) not in pieces:
                pieces[part, q] = window_of(both, 192 * part + 24 * q)
            blocks[16 * q + j] = jnp.where(lane < 24, pieces[part, q], rest).astype(BF)


def at_cells(kept, terms, w_key, w_value, standard, inverse, early, windows):
    channels = standard.shape[1]
    return pl.pallas_call(
        cells_kernel,
        out_shape=[
            jax.ShapeDtypeStruct((8, channels), F32),
            jax.ShapeDtypeStruct((128, 8, LANES), BF),
        ],
        cost_estimate=pl.CostEstimate(flops=30_000_000, bytes_accessed=3_500_000, transcendentals=0),
        name="at_cells",
    )(kept, terms, w_key, w_value, standard, inverse, early, windows)


def pieces_kernel(flags, got, blocks, near, far, placed, conv):
    piece = jnp.sum(got[...].astype(F32), axis=0).astype(BF)
    conv[...] = jnp.sum(blocks[...].astype(F32), axis=0)
    total = jnp.zeros((LANES, piece.shape[1]), F32)
    for i in range(8):
        row = jnp.bitwise_xor(flags[6], i)
        own = blocks[pl.ds(row * 16, 16)].reshape(128, LANES)
        total = total + contract_first(own, near[i] if i < 4 else far[i - 4])
    cell_piece = total[:24].astype(BF)
    odd = flags[4] == 1
    first = jnp.where(odd, cell_piece, piece)
    second = jnp.where(odd, piece, cell_piece)
    for q in range(8):
        placed[q] = first
        placed[8 + q] = second


def pieces(flags, got, blocks, near, far):
    half = near.shape[2]
    vmem = pl.BlockSpec(memory_space=pltpu.VMEM)
    return pl.pallas_call(
        pieces_kernel,
        in_specs=[SCALARS, vmem, vmem, vmem, vmem],
        out_shape=[
            jax.ShapeDtypeStruct((16, 24, half), BF),
            jax.ShapeDtypeStruct((8, LANES), F32),
        ],
        cost_estimate=pl.CostEstimate(flops=100_000_000, bytes_accessed=2_500_000, transcendentals=0),
        name="pieces",
    )(flags, got, blocks, near, far)


def unmix_kernel(flags, early, pooled, top, bottom, left, right, taps, image, padded):
    put_sides(padded, flags, top, bottom, left, right)
    for row in range(16):
        for cell in range(4):
            place = 4 * (row // POOL) + cell
            at = slice(8 * cell, 8 * cell + 8)
            padded[row + 1, 8 + 8 * cell : 16 + 8 * cell, :] = (
                early[row, at, :] + pooled[place : place + 1, :]
            )
    weights = taps[...]
    for row in range(16):
        total = padded[row + 1, 8:40, :]
        for a in range(3):
            for b in range(3):
                tap = 3 * a + b
                total = total + weights[tap : tap + 1] * padded[row + 2 - a, 9 - b : 41 - b, :]
        image[row] = total.astype(BF)


def unmix(flags, early, pooled, sides, taps):
    height, width, channels = early.shape
    block = pl.BlockSpec((height, width, LANES), lambda i: (0, 0, i))
    return pl.pallas_call(
        unmix_kernel,
        grid=(channels // LANES,),
        in_specs=[
            SCALARS,
            block,
            pl.BlockSpec((8, LANES), lambda i: (0, i)),
            *side_specs(),
            pl.BlockSpec((9, LANES), lambda i: (0, i)),
        ],
        out_specs=block,
        out_shape=jax.ShapeDtypeStruct((height, width, channels), BF),
        scratch_shapes=[pltpu.VMEM((18, 48, LANES), F32)],
        cost_estimate=pl.CostEstimate(flops=8_000_000, bytes_accessed=3_000_000, transcendentals=0),
        name="unmix",
    )(flags, early, pooled, *sides, taps)


def block_gradients(image, conv_taps, w_query, w_key, w_value, w_out, grad_out):
    height, width, channels = image.shape
    half = channels // 2
    at_row, at_col = lax.axis_index("row"), lax.axis_index("col")
    core = at_col % 2
    is_first, is_last = at_row == 0, at_row == lax.axis_size("row") - 1
    turned = (core == 1) ^ ((at_col >= 4) & (at_col < 12))
    flags = jnp.stack(
        [
            ~is_first,
            ~is_last,
            at_col > 0,
            at_col < lax.axis_size("col") - 1,
            turned,
            core == 1,
        ]
    ).astype(jnp.int32)
    flags = jnp.concatenate([flags, at_row[None].astype(jnp.int32)])
    flat_grad = grad_out.reshape(-1, channels)
    sides = edges_of(image, is_first, is_last)
    dout = contract_last(flat_grad, w_out).astype(BF)
    hidden, standard, inverse, normed = mix(flags, image, sides, conv_taps)
    cells = lax.all_to_all(normed, "col", 0, 0, tiled=True)
    cells = cells.reshape(-1, channels)
    query = jnp.dot(hidden, w_query, preferred_element_type=F32).astype(BF)
    near = lax.dynamic_slice_in_dim(cells, core * half, half, axis=1)[None]
    for step in range(3):
        far = lax.ppermute(near, "row", [(i, i ^ (1 << step)) for i in range(8)])
        if step < 2:
            near = jnp.concatenate([near, far], axis=0)
    attended, grad_query, kept, sent = attend(flags, query, dout, cells, w_key, w_value)
    theirs = weight_terms((1 - core)[None], grad_query, flat_grad, hidden, attended)
    theirs = lax.ppermute(theirs, "col", PAIRS)
    chip = weight_terms(core[None], grad_query, flat_grad, hidden, attended, theirs)
    got = lax.all_to_all(
        chip.reshape(64, 24, half), BOTH, 0, 0, tiled=True, axis_index_groups=SUM_GROUPS
    )
    terms = lax.ppermute(sent, "col", PAIRS)
    for bit in (1, 2, 3):
        mine = (at_col >> bit) & 1
        total = (kept + terms.astype(F32)).reshape(-1, 2, 2, 8, channels)
        kept = lax.dynamic_index_in_dim(total, mine, 1, keepdims=False)
        sent = lax.dynamic_index_in_dim(total, 1 - mine, 1, keepdims=False).astype(BF)
        terms = lax.ppermute(sent, "col", [(j, j ^ (1 << bit)) for j in range(16)])
    kept, terms = kept[0], terms[0]
    grad_hidden = contract_last(grad_query, w_query)
    early = (flat_grad.astype(F32) + grad_hidden).reshape(height, width, channels)
    early_terms, windows = tap_terms(flags, image, sides, early)
    pooled, block = at_cells(kept, terms, w_key, w_value, standard, inverse, early_terms, windows)
    block, got = lax.optimization_barrier((block, got))
    blocks = lax.all_to_all(block, BOTH, 0, 0, tiled=True)
    rows = jnp.repeat(pooled, POOL, axis=0).reshape(2, width, channels)
    up = jnp.concatenate([pooled[0:1], pooled[4:5]], axis=0)
    down = jnp.concatenate([pooled[3:4], pooled[7:8]], axis=0)
    top, bottom = from_both_sides(
        (early[0] + rows[0]).astype(BF), (early[-1] + rows[1]).astype(BF), "row"
    )
    first = (early[:, 0] + jnp.repeat(up, POOL, axis=0)).astype(BF)
    last = (early[:, -1] + jnp.repeat(down, POOL, axis=0)).astype(BF)
    over = jnp.where(is_first, 0, top).astype(BF)
    under = jnp.where(is_last, 0, bottom).astype(BF)
    left, right = from_both_sides(
        jnp.concatenate([over[:1], first, under[:1]], axis=0),
        jnp.concatenate([over[-1:], last, under[-1:]], axis=0),
        "col",
    )
    grad_image = unmix(flags, early, pooled, (top, bottom, left, right), conv_taps)
    placed, conv = pieces(flags, got, blocks, near, far)
    placed = lax.all_to_all(
        placed, BOTH, 0, 0, tiled=True, axis_index_groups=PLACE_GROUPS
    )
    grad_weights = jnp.transpose(placed.reshape(2, 192, half), (0, 2, 1)).reshape(channels, 192)
    grad_conv = jnp.concatenate([conv[:, 24:72], conv[:1, 72:120]], axis=0)
    return (grad_image, grad_weights.astype(F32), grad_conv)


def solution(mesh):
    return jax.shard_map(
        block_gradients,
        mesh=mesh,
        in_specs=(P("row", "col", None), P(), P(), P(), P(), P(), P("row", "col", None)),
        out_specs=(P("row", "col", None), P(None, "col"), P(None, "col")),
        check_vma=False,
    )
```

```python
import jax
import jax.numpy as jnp
from jax import lax
from jax.experimental import pallas as pl
from jax.experimental.pallas import tpu as pltpu
from jax.sharding import PartitionSpec as P

HD = 64
POOL = 8
EPSILON = 1e-05
BF = jnp.bfloat16
F32 = jnp.float32
LANES = 128
WIDE = 256

FINAL = (0, 1, 2, 3, 12, 13, 14, 15)
PARTNER = (5, 4, 7, 6, 9, 8, 11, 10)
SLICE_AT = tuple((FINAL.index(j) if j in FINAL else PARTNER.index(j)) for j in range(16))
PAIRS = [(j, j ^ 1) for j in range(16)]
BOTH = ("row", "col")


def holder(piece, core):
    return FINAL[piece] if FINAL[piece] % 2 == core else PARTNER[piece]


SUM_GROUPS = [[q * 16 + holder(s, c) for s in range(8) for q in range(8)] for c in range(2)]
PLACE_GROUPS = [[q * 16 + holder(s, c) for c in range(2) for q in range(8)] for s in range(8)]


def from_both_sides(first, last, axis):
    count = lax.axis_size(axis)
    before = lax.ppermute(last, axis, [(i, (i + 1) % count) for i in range(count)])
    after = lax.ppermute(first, axis, [((i + 1) % count, i) for i in range(count)])
    return before, after


def edges_of(tile, is_first, is_last):
    top, bottom = from_both_sides(tile[0], tile[-1], "row")
    up = jnp.where(is_first, 0, top).astype(BF)
    down = jnp.where(is_last, 0, bottom).astype(BF)
    first = jnp.concatenate([up[:1], tile[:, 0], down[:1]], axis=0)
    last = jnp.concatenate([up[-1:], tile[:, -1], down[-1:]], axis=0)
    left, right = from_both_sides(first, last, "col")
    return top, bottom, left, right


def dot(left, right, dims):
    return lax.dot_general(left, right, ((dims[0], dims[1]), ((), ())), preferred_element_type=F32)


def contract_first(left, right):
    return dot(left, right, ((0,), (0,)))


def contract_last(left, right):
    return dot(left, right, ((1,), (1,)))


def put_sides(padded, flags, top, bottom, left, right):
    padded[0, 8:40, :] = top[...].astype(F32) * flags[0].astype(F32)
    padded[17, 8:40, :] = bottom[...].astype(F32) * flags[1].astype(F32)
    first = left[...].astype(F32) * flags[2].astype(F32)
    last = right[...].astype(F32) * flags[3].astype(F32)
    for row in range(18):
        padded[row, 7:8, :] = first[row : row + 1]
        padded[row, 40:41, :] = last[row : row + 1]


def windows_of(padded, at):
    kept = {}

    def window(row, shift):
        if (row, shift) not in kept:
            kept[row, shift] = padded[row, 7 + shift : 39 + shift, at]
        return kept[row, shift]

    return window


def mix_kernel(
    flags, image, top, bottom, left, right, taps, hidden, standard, inverse, normed, padded, pools
):
    step = pl.program_id(0)
    put_sides(padded, flags, top, bottom, left, right)
    padded[1:17, 8:40, :] = image[...].astype(F32)
    per = WIDE // LANES
    for part in range(per):
        at = slice(part * LANES, (part + 1) * LANES)
        weights = taps[:, at]
        window = windows_of(padded, at)
        for cell_row in range(2):
            column = jnp.zeros((32, LANES), F32)
            for row in range(cell_row * POOL, (cell_row + 1) * POOL):
                total = window(row + 1, 1)
                for a in range(3):
                    for b in range(3):
                        tap = 3 * a + b
                        total = total + weights[tap : tap + 1] * window(row + a, b)
                rounded = total.astype(BF)
                hidden[row * 32 : (row + 1) * 32, at] = rounded
                column = column + rounded.astype(F32)
            for cell in range(4):
                one = jnp.sum(column[cell * POOL : (cell + 1) * POOL], axis=0, keepdims=True)
                place = 4 * cell_row + cell
                pools[step * per + part, place : place + 1, :] = one * (1.0 / (POOL * POOL))

    @pl.when(step == pl.num_programs(0) - 1)
    def _():
        blocks = pools.shape[0]
        scale = 1.0 / (blocks * LANES)
        pooled = [pools[i] for i in range(blocks)]
        centre = sum(jnp.sum(x, axis=1, keepdims=True) for x in pooled) * scale
        moved = [x - centre for x in pooled]
        spread = sum(jnp.sum(x * x, axis=1, keepdims=True) for x in moved) * scale
        factor = lax.rsqrt(spread + EPSILON)
        inverse[...] = jnp.broadcast_to(factor, inverse.shape)
        for i in range(blocks):
            at = slice(i * LANES, (i + 1) * LANES)
            own = moved[i] * factor
            standard[:, at] = own
            normed[:, :, at] = jnp.broadcast_to(own.astype(BF)[None], (16, 8, LANES))


def side_specs():
    return [
        pl.BlockSpec((32, WIDE), lambda i: (0, i)),
        pl.BlockSpec((32, WIDE), lambda i: (0, i)),
        pl.BlockSpec((18, WIDE), lambda i: (0, i)),
        pl.BlockSpec((18, WIDE), lambda i: (0, i)),
    ]


SCALARS = pl.BlockSpec(memory_space=pltpu.SMEM)


def mix(flags, image, sides, taps):
    height, width, channels = image.shape
    return pl.pallas_call(
        mix_kernel,
        grid=(channels // WIDE,),
        in_specs=[
            SCALARS,
            pl.BlockSpec((height, width, WIDE), lambda i: (0, 0, i)),
            *side_specs(),
            pl.BlockSpec((9, WIDE), lambda i: (0, i)),
        ],
        out_specs=[
            pl.BlockSpec((height * width, WIDE), lambda i: (0, i)),
            pl.BlockSpec((8, channels), lambda i: (0, 0)),
            pl.BlockSpec((8, LANES), lambda i: (0, 0)),
            pl.BlockSpec((16, 8, channels), lambda i: (0, 0, 0)),
        ],
        out_shape=[
            jax.ShapeDtypeStruct((height * width, channels), BF),
            jax.ShapeDtypeStruct((8, channels), F32),
            jax.ShapeDtypeStruct((8, LANES), F32),
            jax.ShapeDtypeStruct((16, 8, channels), BF),
        ],
        scratch_shapes=[
            pltpu.VMEM((18, 48, WIDE), F32),
            pltpu.VMEM((channels // LANES, 8, LANES), F32),
        ],
        cost_estimate=pl.CostEstimate(flops=8_000_000, bytes_accessed=2_000_000, transcendentals=0),
        name="mix",
    )(flags, image, *sides, taps)


def attend_kernel(query, dout, cells, w_key, w_value, attended, grad_query, sums):
    low = lax.broadcasted_iota(jnp.int32, (128, LANES), 1) < HD
    all_cells = cells[...]
    zero = jnp.zeros((128, LANES), BF)

    def two_heads(weight):
        both = jnp.dot(all_cells, weight[...], preferred_element_type=F32).astype(BF)
        return jnp.concatenate([jnp.where(low, both, zero), jnp.where(low, zero, both)], axis=0)

    keys = two_heads(w_key) * jnp.asarray(HD**-0.5, BF)
    values = two_heads(w_value)
    q, d = query[...], dout[...]
    expons = jnp.exp(contract_last(keys, q))
    grads = contract_last(values, d)
    probs, scores = [], []
    for head in range(2):
        own = expons[head * 128 : (head + 1) * 128]
        prob = own * (1.0 / jnp.sum(own, axis=0, keepdims=True))
        grad = grads[head * 128 : (head + 1) * 128]
        delta = jnp.sum(prob * grad, axis=0, keepdims=True)
        probs.append(prob.astype(BF))
        scores.append((prob * (grad - delta)).astype(BF))
    weights = jnp.concatenate(probs, axis=0)
    grad_scores = jnp.concatenate(scores, axis=0)
    attended[...] = contract_first(values, weights).astype(BF)
    grad_query[...] = contract_first(keys, grad_scores).astype(BF)
    grad_keys = jnp.dot(grad_scores, q, preferred_element_type=F32)
    grad_values = jnp.dot(weights, d, preferred_element_type=F32)
    grad_keys = jnp.where(low, grad_keys[:128], grad_keys[128:]) * (HD**-0.5)
    grad_values = jnp.where(low, grad_values[:128], grad_values[128:])
    sums[:, 0] = grad_keys.astype(BF).reshape(16, 8, LANES)
    sums[:, 1] = grad_values.astype(BF).reshape(16, 8, LANES)


def attend(query, dout, cells, w_key, w_value):
    tokens, channels = query.shape
    by_pair = pl.BlockSpec((tokens, LANES), lambda i: (0, i))
    turned = pl.BlockSpec((LANES, tokens), lambda i: (i, 0))
    weight = pl.BlockSpec((channels, LANES), lambda i: (0, i))
    return pl.pallas_call(
        attend_kernel,
        grid=(channels // LANES,),
        in_specs=[
            by_pair,
            by_pair,
            pl.BlockSpec((128, channels), lambda i: (0, 0)),
            weight,
            weight,
        ],
        out_specs=[turned, turned, pl.BlockSpec((16, 2, 8, LANES), lambda i: (0, 0, 0, i))],
        out_shape=[
            jax.ShapeDtypeStruct((channels, tokens), BF),
            jax.ShapeDtypeStruct((channels, tokens), BF),
            jax.ShapeDtypeStruct((16, 2, 8, channels), BF),
        ],
        cost_estimate=pl.CostEstimate(
            flops=3_000_000_000, bytes_accessed=6_000_000, transcendentals=800_000
        ),
        name="attend",
    )(query, dout, cells, w_key, w_value)


def taps_kernel(flags, image, top, bottom, left, right, early, terms, windows, padded, lines):
    put_sides(padded, flags, top, bottom, left, right)
    padded[1:17, 8:40, :] = image[...].astype(F32)
    for part in range(WIDE // LANES):
        at = slice(part * LANES, (part + 1) * LANES)
        window = windows_of(padded, at)
        totals = [jnp.zeros((8, LANES), F32) for _ in range(9)]
        for row in range(16):
            grad = early[row, :, at]
            for a in range(3):
                for b in range(3):
                    term = grad * window(row + a, b)
                    totals[3 * a + b] = totals[3 * a + b] + (
                        (term[:8] + term[8:16]) + (term[16:24] + term[24:])
                    )
        for tap in range(9):
            terms[tap : tap + 1, at] = jnp.sum(totals[tap], axis=0, keepdims=True)
    for cell_row in range(2):
        for a in range(3):
            start = cell_row * POOL + a
            line = padded[start]
            for row in range(start + 1, start + POOL):
                line = line + padded[row]
            lines[...] = line
            for b in range(3):
                for cell in range(4):
                    part = lines[7 + b + 8 * cell : 15 + b + 8 * cell, :]
                    place = 4 * cell_row + cell
                    windows[3 * a + b, place : place + 1, :] = jnp.sum(part, axis=0, keepdims=True)


def tap_terms(flags, image, sides, early):
    height, width, channels = image.shape
    block = pl.BlockSpec((height, width, WIDE), lambda i: (0, 0, i))
    return pl.pallas_call(
        taps_kernel,
        grid=(channels // WIDE,),
        in_specs=[SCALARS, block, *side_specs(), block],
        out_specs=[
            pl.BlockSpec((9, WIDE), lambda i: (0, i)),
            pl.BlockSpec((9, 8, WIDE), lambda i: (0, 0, i)),
        ],
        out_shape=[
            jax.ShapeDtypeStruct((9, channels), F32),
            jax.ShapeDtypeStruct((9, 8, channels), F32),
        ],
        scratch_shapes=[pltpu.VMEM((18, 48, WIDE), F32), pltpu.VMEM((48, WIDE), F32)],
        cost_estimate=pl.CostEstimate(flops=8_000_000, bytes_accessed=3_000_000, transcendentals=0),
        name="tap_terms",
    )(flags, image, *sides, early)


def window_of(x, start):
    base = min(start // LANES * LANES, x.shape[1] - 2 * LANES)
    if start == base:
        return x[:, base : base + LANES]
    return pltpu.roll(x[:, base : base + 2 * LANES], base - start + 2 * LANES, 1)[:, :LANES]


def cells_kernel(terms, w_key, w_value, standard, inverse, early, windows, grad_pooled, blocks):
    received = jnp.sum(terms[...].astype(F32), axis=0)
    keys, values = received[0], received[1]
    grad = contract_last(keys.astype(BF), w_key[...]) + contract_last(values.astype(BF), w_value[...])
    own = standard[...]
    scale = 1.0 / own.shape[1]
    centre = jnp.sum(grad, axis=1, keepdims=True) * scale
    along = jnp.sum(grad * own, axis=1, keepdims=True) * scale
    pooled = (grad - centre - own * along) * (inverse[:, :1] * (1.0 / (POOL * POOL)))
    grad_pooled[...] = pooled
    conv = [
        early[t : t + 1, :] + jnp.sum(pooled * windows[t], axis=0, keepdims=True) for t in range(9)
    ]
    first, last = jnp.concatenate(conv[:8], axis=0), jnp.broadcast_to(conv[8], (8, own.shape[1]))
    lane = lax.broadcasted_iota(jnp.int32, (8, LANES), 1)
    both = jnp.concatenate([keys, values], axis=1)
    width = own.shape[1] // 16
    pieces = {}
    for j in range(16):
        part = PARTNER[SLICE_AT[j]] - 4
        taps = pltpu.roll(window_of(first, width * j), 24, 1)
        tail = pltpu.roll(window_of(last, width * j), 72, 1)
        rest = jnp.where(lane < 72, taps, tail)
        for q in range(8):
            if (part, q) not in pieces:
                pieces[part, q] = window_of(both, 192 * part + 24 * q)
            blocks[16 * q + j] = jnp.where(lane < 24, pieces[part, q], rest).astype(BF)


def at_cells(terms, w_key, w_value, standard, inverse, early, windows):
    channels = standard.shape[1]
    return pl.pallas_call(
        cells_kernel,
        out_shape=[
            jax.ShapeDtypeStruct((8, channels), F32),
            jax.ShapeDtypeStruct((128, 8, LANES), BF),
        ],
        cost_estimate=pl.CostEstimate(flops=30_000_000, bytes_accessed=3_500_000, transcendentals=0),
        name="at_cells",
    )(terms, w_key, w_value, standard, inverse, early, windows)


def pieces_kernel(flags, got, blocks, near, far, placed, conv):
    piece = jnp.sum(got[...].astype(F32), axis=0).astype(BF)
    conv[...] = jnp.sum(blocks[...].astype(F32), axis=0)
    total = jnp.zeros((LANES, piece.shape[1]), F32)
    for i in range(8):
        row = jnp.bitwise_xor(flags[5], i)
        own = blocks[pl.ds(row * 16, 16)].reshape(128, LANES)
        total = total + contract_first(own, near[i] if i < 4 else far[i - 4])
    cell_piece = total[:24].astype(BF)
    odd = flags[4] == 1
    first = jnp.where(odd, cell_piece, piece)
    second = jnp.where(odd, piece, cell_piece)
    for q in range(8):
        placed[q] = first
        placed[8 + q] = second


def pieces(flags, got, blocks, near, far):
    half = near.shape[2]
    vmem = pl.BlockSpec(memory_space=pltpu.VMEM)
    return pl.pallas_call(
        pieces_kernel,
        in_specs=[SCALARS, vmem, vmem, vmem, vmem],
        out_shape=[
            jax.ShapeDtypeStruct((16, 24, half), BF),
            jax.ShapeDtypeStruct((8, LANES), F32),
        ],
        cost_estimate=pl.CostEstimate(flops=100_000_000, bytes_accessed=2_500_000, transcendentals=0),
        name="pieces",
    )(flags, got, blocks, near, far)


def unmix_kernel(flags, early, pooled, top, bottom, left, right, taps, image, padded):
    put_sides(padded, flags, top, bottom, left, right)
    for row in range(16):
        for cell in range(4):
            place = 4 * (row // POOL) + cell
            at = slice(8 * cell, 8 * cell + 8)
            padded[row + 1, 8 + 8 * cell : 16 + 8 * cell, :] = (
                early[row, at, :] + pooled[place : place + 1, :]
            )
    for part in range(WIDE // LANES):
        at = slice(part * LANES, (part + 1) * LANES)
        weights = taps[:, at]
        window = windows_of(padded, at)
        for row in range(16):
            total = window(row + 1, 1)
            for a in range(3):
                for b in range(3):
                    tap = 3 * a + b
                    total = total + weights[tap : tap + 1] * window(row + 2 - a, 2 - b)
            image[row, :, at] = total.astype(BF)


def unmix(flags, early, pooled, sides, taps):
    height, width, channels = early.shape
    block = pl.BlockSpec((height, width, WIDE), lambda i: (0, 0, i))
    return pl.pallas_call(
        unmix_kernel,
        grid=(channels // WIDE,),
        in_specs=[
            SCALARS,
            block,
            pl.BlockSpec((8, WIDE), lambda i: (0, i)),
            *side_specs(),
            pl.BlockSpec((9, WIDE), lambda i: (0, i)),
        ],
        out_specs=block,
        out_shape=jax.ShapeDtypeStruct((height, width, channels), BF),
        scratch_shapes=[pltpu.VMEM((18, 48, WIDE), F32)],
        cost_estimate=pl.CostEstimate(flops=8_000_000, bytes_accessed=3_000_000, transcendentals=0),
        name="unmix",
    )(flags, early, pooled, *sides, taps)


def block_gradients(image, conv_taps, w_query, w_key, w_value, w_out, grad_out):
    height, width, channels = image.shape
    half = channels // 2
    at_row, at_col = lax.axis_index("row"), lax.axis_index("col")
    core = at_col % 2
    is_first, is_last = at_row == 0, at_row == lax.axis_size("row") - 1
    turned = (core == 1) ^ ((at_col >= 4) & (at_col < 12))
    flags = jnp.stack(
        [
            ~is_first,
            ~is_last,
            at_col > 0,
            at_col < lax.axis_size("col") - 1,
            turned,
        ]
    ).astype(jnp.int32)
    flags = jnp.concatenate([flags, at_row[None].astype(jnp.int32)])
    flat_grad = grad_out.reshape(-1, channels)
    sides = edges_of(image, is_first, is_last)
    dout = contract_last(flat_grad, w_out).astype(BF)
    hidden, standard, inverse, normed = mix(flags, image, sides, conv_taps)
    cells = lax.all_to_all(normed, "col", 0, 0, tiled=True)
    cells = cells.reshape(-1, channels)
    query = jnp.dot(hidden, w_query, preferred_element_type=F32).astype(BF)
    near = lax.dynamic_slice_in_dim(cells, core * half, half, axis=1)[None]
    for step in range(3):
        far = lax.ppermute(near, "row", [(i, i ^ (1 << step)) for i in range(8)])
        if step < 2:
            near = jnp.concatenate([near, far], axis=0)
    attended, grad_query, sums = attend(query, dout, cells, w_key, w_value)
    terms = lax.all_to_all(sums, "col", 0, 0, tiled=True)

    def half_terms(which):
        h = lax.dynamic_slice_in_dim(hidden, which * half, half, axis=1)
        a = lax.dynamic_slice_in_dim(attended, which * half, half, axis=0)
        return (
            dot(grad_query, h, ((1,), (0,))).astype(BF),
            dot(flat_grad, a, ((0,), (1,))).astype(BF),
        )

    sent = half_terms(1 - core)
    theirs = [lax.ppermute(x, "col", PAIRS) for x in sent]
    own = lax.optimization_barrier(half_terms(core))
    chip = jnp.concatenate(
        [x.astype(F32) + y.astype(F32) for x, y in zip(own, theirs)], axis=0
    ).astype(BF)
    chip, terms = lax.optimization_barrier((chip, terms))
    got = lax.all_to_all(
        chip.reshape(64, 24, half), BOTH, 0, 0, tiled=True, axis_index_groups=SUM_GROUPS
    )
    grad_hidden = dot(grad_query, w_query, ((0,), (1,)))
    early = (flat_grad.astype(F32) + grad_hidden).reshape(height, width, channels)
    early_terms, windows = tap_terms(flags, image, sides, early)
    pooled, block = at_cells(
        terms, w_key, w_value, standard, inverse, early_terms, windows
    )
    block, got = lax.optimization_barrier((block, got))
    blocks = lax.all_to_all(block, BOTH, 0, 0, tiled=True)
    rows = jnp.repeat(pooled, POOL, axis=0).reshape(2, width, channels)
    up = jnp.concatenate([pooled[0:1], pooled[4:5]], axis=0)
    down = jnp.concatenate([pooled[3:4], pooled[7:8]], axis=0)
    top, bottom = from_both_sides(
        (early[0] + rows[0]).astype(BF), (early[-1] + rows[1]).astype(BF), "row"
    )
    first = (early[:, 0] + jnp.repeat(up, POOL, axis=0)).astype(BF)
    last = (early[:, -1] + jnp.repeat(down, POOL, axis=0)).astype(BF)
    over = jnp.where(is_first, 0, top).astype(BF)
    under = jnp.where(is_last, 0, bottom).astype(BF)
    left, right = from_both_sides(
        jnp.concatenate([over[:1], first, under[:1]], axis=0),
        jnp.concatenate([over[-1:], last, under[-1:]], axis=0),
        "col",
    )
    grad_image = unmix(flags, early, pooled, (top, bottom, left, right), conv_taps)
    placed, conv = pieces(flags, got, blocks, near, far)
    placed = lax.all_to_all(
        placed, BOTH, 0, 0, tiled=True, axis_index_groups=PLACE_GROUPS
    )
    grad_weights = jnp.transpose(placed.reshape(2, 192, half), (0, 2, 1)).reshape(channels, 192)
    grad_conv = jnp.concatenate([conv[:, 24:72], conv[:1, 72:120]], axis=0)
    return (grad_image, grad_weights.astype(F32), grad_conv)


def solution(mesh):
    return jax.shard_map(
        block_gradients,
        mesh=mesh,
        in_specs=(P("row", "col", None), P(), P(), P(), P(), P(), P("row", "col", None)),
        out_specs=(P("row", "col", None), P(None, "col"), P(None, "col")),
        check_vma=False,
    )
```

```python
import jax
import jax.numpy as jnp
from jax import lax
from jax.experimental import pallas as pl
from jax.experimental.pallas import tpu as pltpu
from jax.sharding import PartitionSpec as P

HD = 64
POOL = 8
EPSILON = 1e-05
BF = jnp.bfloat16
F32 = jnp.float32
LANES = 128
WIDE = 256

FINAL = (0, 1, 2, 3, 12, 13, 14, 15)
PARTNER = (5, 4, 7, 6, 9, 8, 11, 10)
SLICE_AT = tuple((FINAL.index(j) if j in FINAL else PARTNER.index(j)) for j in range(16))
PAIRS = [(j, j ^ 1) for j in range(16)]
OTHER_PAIRS = [(j, (j + (1 if j % 2 else -1)) % 16) for j in range(16)]
BOTH = ("row", "col")


def holder(piece, core):
    return FINAL[piece] if FINAL[piece] % 2 == core else PARTNER[piece]


SUM_GROUPS = [[q * 16 + holder(s, c) for s in range(8) for q in range(8)] for c in range(2)]
PLACE_GROUPS = [[q * 16 + holder(s, c) for c in range(2) for q in range(8)] for s in range(8)]


def from_both_sides(first, last, axis):
    count = lax.axis_size(axis)
    before = lax.ppermute(last, axis, [(i, (i + 1) % count) for i in range(count)])
    after = lax.ppermute(first, axis, [((i + 1) % count, i) for i in range(count)])
    return before, after


def column_sides(first, last):
    odd = lax.axis_index("col") % 2 == 1
    near = lax.ppermute(jnp.where(odd, first, last), "col", PAIRS)
    far = lax.ppermute(jnp.where(odd, last, first), "col", OTHER_PAIRS)
    return jnp.where(odd, near, far), jnp.where(odd, far, near)


def edges_of(tile, is_first, is_last):
    top, bottom = from_both_sides(tile[0], tile[-1], "row")
    up = jnp.where(is_first, 0, top).astype(BF)
    down = jnp.where(is_last, 0, bottom).astype(BF)
    first = jnp.concatenate([up[:1], tile[:, 0], down[:1]], axis=0)
    last = jnp.concatenate([up[-1:], tile[:, -1], down[-1:]], axis=0)
    left, right = column_sides(first, last)
    return top, bottom, left, right


def dot(left, right, dims):
    return lax.dot_general(left, right, ((dims[0], dims[1]), ((), ())), preferred_element_type=F32)


def contract_first(left, right):
    return dot(left, right, ((0,), (0,)))


def contract_last(left, right):
    return dot(left, right, ((1,), (1,)))


def put_sides(padded, flags, top, bottom, left, right):
    padded[0, 8:40, :] = top[...].astype(F32) * flags[0].astype(F32)
    padded[17, 8:40, :] = bottom[...].astype(F32) * flags[1].astype(F32)
    first = left[...].astype(F32) * flags[2].astype(F32)
    last = right[...].astype(F32) * flags[3].astype(F32)
    for row in range(18):
        padded[row, 7:8, :] = first[row : row + 1]
        padded[row, 40:41, :] = last[row : row + 1]


def windows_of(padded, at):
    kept = {}

    def window(row, shift):
        if (row, shift) not in kept:
            kept[row, shift] = padded[row, 7 + shift : 39 + shift, at]
        return kept[row, shift]

    return window


def mix_kernel(
    flags, image, top, bottom, left, right, taps, hidden, standard, inverse, normed, padded, pools
):
    step = pl.program_id(0)
    put_sides(padded, flags, top, bottom, left, right)
    padded[1:17, 8:40, :] = image[...].astype(F32)
    per = WIDE // LANES
    for part in range(per):
        at = slice(part * LANES, (part + 1) * LANES)
        weights = taps[:, at]
        window = windows_of(padded, at)
        for cell_row in range(2):
            column = jnp.zeros((32, LANES), F32)
            for row in range(cell_row * POOL, (cell_row + 1) * POOL):
                total = window(row + 1, 1)
                for a in range(3):
                    for b in range(3):
                        tap = 3 * a + b
                        total = total + weights[tap : tap + 1] * window(row + a, b)
                rounded = total.astype(BF)
                hidden[row * 32 : (row + 1) * 32, at] = rounded
                column = column + rounded.astype(F32)
            for cell in range(4):
                one = jnp.sum(column[cell * POOL : (cell + 1) * POOL], axis=0, keepdims=True)
                place = 4 * cell_row + cell
                pools[step * per + part, place : place + 1, :] = one * (1.0 / (POOL * POOL))

    @pl.when(step == pl.num_programs(0) - 1)
    def _():
        blocks = pools.shape[0]
        scale = 1.0 / (blocks * LANES)
        pooled = [pools[i] for i in range(blocks)]
        centre = sum(jnp.sum(x, axis=1, keepdims=True) for x in pooled) * scale
        moved = [x - centre for x in pooled]
        spread = sum(jnp.sum(x * x, axis=1, keepdims=True) for x in moved) * scale
        factor = lax.rsqrt(spread + EPSILON)
        inverse[...] = jnp.broadcast_to(factor, inverse.shape)
        for i in range(blocks):
            at = slice(i * LANES, (i + 1) * LANES)
            own = moved[i] * factor
            standard[:, at] = own
            normed[:, :, at] = jnp.broadcast_to(own.astype(BF)[None], (16, 8, LANES))


def side_specs():
    return [
        pl.BlockSpec((32, WIDE), lambda i: (0, i)),
        pl.BlockSpec((32, WIDE), lambda i: (0, i)),
        pl.BlockSpec((18, WIDE), lambda i: (0, i)),
        pl.BlockSpec((18, WIDE), lambda i: (0, i)),
    ]


SCALARS = pl.BlockSpec(memory_space=pltpu.SMEM)


def mix(flags, image, sides, taps):
    height, width, channels = image.shape
    return pl.pallas_call(
        mix_kernel,
        grid=(channels // WIDE,),
        in_specs=[
            SCALARS,
            pl.BlockSpec((height, width, WIDE), lambda i: (0, 0, i)),
            *side_specs(),
            pl.BlockSpec((9, WIDE), lambda i: (0, i)),
        ],
        out_specs=[
            pl.BlockSpec((height * width, WIDE), lambda i: (0, i)),
            pl.BlockSpec((8, channels), lambda i: (0, 0)),
            pl.BlockSpec((8, LANES), lambda i: (0, 0)),
            pl.BlockSpec((16, 8, channels), lambda i: (0, 0, 0)),
        ],
        out_shape=[
            jax.ShapeDtypeStruct((height * width, channels), BF),
            jax.ShapeDtypeStruct((8, channels), F32),
            jax.ShapeDtypeStruct((8, LANES), F32),
            jax.ShapeDtypeStruct((16, 8, channels), BF),
        ],
        scratch_shapes=[
            pltpu.VMEM((18, 48, WIDE), F32),
            pltpu.VMEM((channels // LANES, 8, LANES), F32),
        ],
        compiler_params=pltpu.CompilerParams(vmem_limit_bytes=16 << 20),
        cost_estimate=pl.CostEstimate(flops=8_000_000, bytes_accessed=2_000_000, transcendentals=0),
        name="mix",
    )(flags, image, *sides, taps)


def attend_kernel(query, dout, cells, w_key, w_value, attended, grad_query, sums):
    low = lax.broadcasted_iota(jnp.int32, (128, LANES), 1) < HD
    all_cells = cells[...]
    zero = jnp.zeros((128, LANES), BF)

    def two_heads(weight):
        both = jnp.dot(all_cells, weight[...], preferred_element_type=F32).astype(BF)
        return jnp.concatenate([jnp.where(low, both, zero), jnp.where(low, zero, both)], axis=0)

    keys = two_heads(w_key) * jnp.asarray(HD**-0.5, BF)
    values = two_heads(w_value)
    q, d = query[...], dout[...]
    expons = jnp.exp(contract_last(keys, q))
    grads = contract_last(values, d)
    probs, scores = [], []
    for head in range(2):
        own = expons[head * 128 : (head + 1) * 128]
        prob = own * (1.0 / jnp.sum(own, axis=0, keepdims=True))
        grad = grads[head * 128 : (head + 1) * 128]
        delta = jnp.sum(prob * grad, axis=0, keepdims=True)
        probs.append(prob.astype(BF))
        scores.append((prob * (grad - delta)).astype(BF))
    weights = jnp.concatenate(probs, axis=0)
    grad_scores = jnp.concatenate(scores, axis=0)
    attended[...] = contract_first(values, weights).astype(BF)
    grad_query[...] = contract_first(keys, grad_scores).astype(BF)
    grad_keys = jnp.dot(grad_scores, q, preferred_element_type=F32)
    grad_values = jnp.dot(weights, d, preferred_element_type=F32)
    grad_keys = jnp.where(low, grad_keys[:128], grad_keys[128:]) * (HD**-0.5)
    grad_values = jnp.where(low, grad_values[:128], grad_values[128:])
    sums[:, 0] = grad_keys.astype(BF).reshape(16, 8, LANES)
    sums[:, 1] = grad_values.astype(BF).reshape(16, 8, LANES)


def attend(query, dout, cells, w_key, w_value):
    tokens, channels = query.shape
    by_pair = pl.BlockSpec((tokens, LANES), lambda i: (0, i))
    turned = pl.BlockSpec((LANES, tokens), lambda i: (i, 0))
    weight = pl.BlockSpec((channels, LANES), lambda i: (0, i))
    return pl.pallas_call(
        attend_kernel,
        grid=(channels // LANES,),
        in_specs=[
            by_pair,
            by_pair,
            pl.BlockSpec((128, channels), lambda i: (0, 0)),
            weight,
            weight,
        ],
        out_specs=[turned, turned, pl.BlockSpec((16, 2, 8, LANES), lambda i: (0, 0, 0, i))],
        out_shape=[
            jax.ShapeDtypeStruct((channels, tokens), BF),
            jax.ShapeDtypeStruct((channels, tokens), BF),
            jax.ShapeDtypeStruct((16, 2, 8, channels), BF),
        ],
        cost_estimate=pl.CostEstimate(
            flops=3_000_000_000, bytes_accessed=6_000_000, transcendentals=800_000
        ),
        name="attend",
    )(query, dout, cells, w_key, w_value)


def chip_kernel(own_query, their_query, own_out, their_out, chip):
    chip[0] = (own_query[...].astype(F32) + their_query[...].astype(F32)).astype(BF)
    chip[1] = (own_out[...].astype(F32) + their_out[...].astype(F32)).astype(BF)


def chip_sums(own, theirs):
    rows, half = own[0].shape
    block = pl.BlockSpec((rows // 2, half), lambda i: (i, 0))
    return pl.pallas_call(
        chip_kernel,
        grid=(2,),
        in_specs=[block] * 4,
        out_specs=pl.BlockSpec((2, rows // 2, half), lambda i: (0, i, 0)),
        out_shape=jax.ShapeDtypeStruct((2, rows, half), BF),
        compiler_params=pltpu.CompilerParams(vmem_limit_bytes=16 << 20),
        cost_estimate=pl.CostEstimate(flops=1_200_000, bytes_accessed=3_500_000, transcendentals=0),
        name="chip_sums",
    )(own[0], theirs[0], own[1], theirs[1])


def taps_kernel(flags, image, top, bottom, left, right, early, terms, windows, padded, lines):
    put_sides(padded, flags, top, bottom, left, right)
    padded[1:17, 8:40, :] = image[...].astype(F32)
    for part in range(WIDE // LANES):
        at = slice(part * LANES, (part + 1) * LANES)
        window = windows_of(padded, at)
        totals = [jnp.zeros((8, LANES), F32) for _ in range(9)]
        for row in range(16):
            grad = early[row, :, at]
            for a in range(3):
                for b in range(3):
                    term = grad * window(row + a, b)
                    totals[3 * a + b] = totals[3 * a + b] + (
                        (term[:8] + term[8:16]) + (term[16:24] + term[24:])
                    )
        for tap in range(9):
            terms[tap : tap + 1, at] = jnp.sum(totals[tap], axis=0, keepdims=True)
    for cell_row in range(2):
        for a in range(3):
            start = cell_row * POOL + a
            line = padded[start]
            for row in range(start + 1, start + POOL):
                line = line + padded[row]
            lines[...] = line
            for b in range(3):
                for cell in range(4):
                    part = lines[7 + b + 8 * cell : 15 + b + 8 * cell, :]
                    place = 4 * cell_row + cell
                    windows[3 * a + b, place : place + 1, :] = jnp.sum(part, axis=0, keepdims=True)


def tap_terms(flags, image, sides, early):
    height, width, channels = image.shape
    block = pl.BlockSpec((height, width, WIDE), lambda i: (0, 0, i))
    return pl.pallas_call(
        taps_kernel,
        grid=(channels // WIDE,),
        in_specs=[SCALARS, block, *side_specs(), block],
        out_specs=[
            pl.BlockSpec((9, WIDE), lambda i: (0, i)),
            pl.BlockSpec((9, 8, WIDE), lambda i: (0, 0, i)),
        ],
        out_shape=[
            jax.ShapeDtypeStruct((9, channels), F32),
            jax.ShapeDtypeStruct((9, 8, channels), F32),
        ],
        scratch_shapes=[pltpu.VMEM((18, 48, WIDE), F32), pltpu.VMEM((48, WIDE), F32)],
        compiler_params=pltpu.CompilerParams(vmem_limit_bytes=16 << 20),
        cost_estimate=pl.CostEstimate(flops=8_000_000, bytes_accessed=3_000_000, transcendentals=0),
        name="tap_terms",
    )(flags, image, *sides, early)


def window_of(x, start):
    base = min(start // LANES * LANES, x.shape[1] - 2 * LANES)
    if start == base:
        return x[:, base : base + LANES]
    return pltpu.roll(x[:, base : base + 2 * LANES], base - start + 2 * LANES, 1)[:, :LANES]


def cells_kernel(terms, w_key, w_value, standard, inverse, early, windows, grad_pooled, blocks):
    received = jnp.sum(terms[...].astype(F32), axis=0)
    keys, values = received[0], received[1]
    grad = contract_last(keys.astype(BF), w_key[...]) + contract_last(values.astype(BF), w_value[...])
    own = standard[...]
    scale = 1.0 / own.shape[1]
    centre = jnp.sum(grad, axis=1, keepdims=True) * scale
    along = jnp.sum(grad * own, axis=1, keepdims=True) * scale
    pooled = (grad - centre - own * along) * (inverse[:, :1] * (1.0 / (POOL * POOL)))
    grad_pooled[...] = pooled
    conv = [
        early[t : t + 1, :] + jnp.sum(pooled * windows[t], axis=0, keepdims=True) for t in range(9)
    ]
    first, last = jnp.concatenate(conv[:8], axis=0), jnp.broadcast_to(conv[8], (8, own.shape[1]))
    lane = lax.broadcasted_iota(jnp.int32, (8, LANES), 1)
    both = jnp.concatenate([keys, values], axis=1)
    width = own.shape[1] // 16
    pieces = {}
    for j in range(16):
        part = PARTNER[SLICE_AT[j]] - 4
        taps = pltpu.roll(window_of(first, width * j), 24, 1)
        tail = pltpu.roll(window_of(last, width * j), 72, 1)
        rest = jnp.where(lane < 72, taps, tail)
        for q in range(8):
            if (part, q) not in pieces:
                pieces[part, q] = window_of(both, 192 * part + 24 * q)
            blocks[16 * q + j] = jnp.where(lane < 24, pieces[part, q], rest).astype(BF)


def at_cells(terms, w_key, w_value, standard, inverse, early, windows):
    channels = standard.shape[1]
    return pl.pallas_call(
        cells_kernel,
        out_shape=[
            jax.ShapeDtypeStruct((8, channels), F32),
            jax.ShapeDtypeStruct((128, 8, LANES), BF),
        ],
        compiler_params=pltpu.CompilerParams(vmem_limit_bytes=16 << 20),
        cost_estimate=pl.CostEstimate(flops=30_000_000, bytes_accessed=3_500_000, transcendentals=0),
        name="at_cells",
    )(terms, w_key, w_value, standard, inverse, early, windows)


def pieces_kernel(flags, got, blocks, near, far, placed, conv):
    piece = jnp.sum(got[...].astype(F32), axis=0).astype(BF)
    conv[...] = jnp.sum(blocks[...].astype(F32), axis=0)
    total = jnp.zeros((LANES, piece.shape[1]), F32)
    for i in range(8):
        row = jnp.bitwise_xor(flags[5], i)
        own = blocks[pl.ds(row * 16, 16)].reshape(128, LANES)
        total = total + contract_first(own, near[i] if i < 4 else far[i - 4])
    cell_piece = total[:24].astype(BF)
    odd = flags[4] == 1
    first = jnp.where(odd, cell_piece, piece)
    second = jnp.where(odd, piece, cell_piece)
    for q in range(8):
        placed[q] = first
        placed[8 + q] = second


def pieces(flags, got, blocks, near, far):
    half = near.shape[2]
    vmem = pl.BlockSpec(memory_space=pltpu.VMEM)
    return pl.pallas_call(
        pieces_kernel,
        in_specs=[SCALARS, vmem, vmem, vmem, vmem],
        out_shape=[
            jax.ShapeDtypeStruct((16, 24, half), BF),
            jax.ShapeDtypeStruct((8, LANES), F32),
        ],
        compiler_params=pltpu.CompilerParams(vmem_limit_bytes=16 << 20),
        cost_estimate=pl.CostEstimate(flops=100_000_000, bytes_accessed=2_500_000, transcendentals=0),
        name="pieces",
    )(flags, got, blocks, near, far)


def unmix_kernel(flags, early, pooled, top, bottom, left, right, taps, image, padded):
    put_sides(padded, flags, top, bottom, left, right)
    for row in range(16):
        for cell in range(4):
            place = 4 * (row // POOL) + cell
            at = slice(8 * cell, 8 * cell + 8)
            padded[row + 1, 8 + 8 * cell : 16 + 8 * cell, :] = (
                early[row, at, :] + pooled[place : place + 1, :]
            )
    for part in range(WIDE // LANES):
        at = slice(part * LANES, (part + 1) * LANES)
        weights = taps[:, at]
        window = windows_of(padded, at)
        for row in range(16):
            total = window(row + 1, 1)
            for a in range(3):
                for b in range(3):
                    tap = 3 * a + b
                    total = total + weights[tap : tap + 1] * window(row + 2 - a, 2 - b)
            image[row, :, at] = total.astype(BF)


def unmix(flags, early, pooled, sides, taps):
    height, width, channels = early.shape
    block = pl.BlockSpec((height, width, WIDE), lambda i: (0, 0, i))
    return pl.pallas_call(
        unmix_kernel,
        grid=(channels // WIDE,),
        in_specs=[
            SCALARS,
            block,
            pl.BlockSpec((8, WIDE), lambda i: (0, i)),
            *side_specs(),
            pl.BlockSpec((9, WIDE), lambda i: (0, i)),
        ],
        out_specs=block,
        out_shape=jax.ShapeDtypeStruct((height, width, channels), BF),
        scratch_shapes=[pltpu.VMEM((18, 48, WIDE), F32)],
        compiler_params=pltpu.CompilerParams(vmem_limit_bytes=16 << 20),
        cost_estimate=pl.CostEstimate(flops=8_000_000, bytes_accessed=3_000_000, transcendentals=0),
        name="unmix",
    )(flags, early, pooled, *sides, taps)


def block_gradients(image, conv_taps, w_query, w_key, w_value, w_out, grad_out):
    height, width, channels = image.shape
    half = channels // 2
    at_row, at_col = lax.axis_index("row"), lax.axis_index("col")
    core = at_col % 2
    is_first, is_last = at_row == 0, at_row == lax.axis_size("row") - 1
    turned = (core == 1) ^ ((at_col >= 4) & (at_col < 12))
    flags = jnp.stack(
        [
            ~is_first,
            ~is_last,
            at_col > 0,
            at_col < lax.axis_size("col") - 1,
            turned,
        ]
    ).astype(jnp.int32)
    flags = jnp.concatenate([flags, at_row[None].astype(jnp.int32)])
    flat_grad = grad_out.reshape(-1, channels)
    sides = edges_of(image, is_first, is_last)
    dout = contract_last(flat_grad, w_out).astype(BF)
    hidden, standard, inverse, normed = mix(flags, image, sides, conv_taps)
    cells = lax.all_to_all(normed, "col", 0, 0, tiled=True)
    cells = cells.reshape(-1, channels)
    query = jnp.dot(hidden, w_query, preferred_element_type=F32).astype(BF)
    near = lax.dynamic_slice_in_dim(cells, core * half, half, axis=1)[None]
    for step in range(3):
        far = lax.ppermute(near, "row", [(i, i ^ (1 << step)) for i in range(8)])
        if step < 2:
            near = jnp.concatenate([near, far], axis=0)
    attended, grad_query, sums = attend(query, dout, cells, w_key, w_value)
    terms = lax.all_to_all(sums, "col", 0, 0, tiled=True)

    def half_terms(which):
        h = lax.dynamic_slice_in_dim(hidden, which * half, half, axis=1)
        a = lax.dynamic_slice_in_dim(attended, which * half, half, axis=0)
        return (
            dot(grad_query, h, ((1,), (0,))).astype(BF),
            dot(flat_grad, a, ((0,), (1,))).astype(BF),
        )

    sent = half_terms(1 - core)
    theirs = [lax.ppermute(x, "col", PAIRS) for x in sent]
    own = lax.optimization_barrier(half_terms(core))
    chip = chip_sums(own, theirs)
    chip, terms = lax.optimization_barrier((chip, terms))
    got = lax.all_to_all(
        chip.reshape(64, 24, half), BOTH, 0, 0, tiled=True, axis_index_groups=SUM_GROUPS
    )
    grad_hidden = dot(grad_query, w_query, ((0,), (1,)))
    early = (flat_grad.astype(F32) + grad_hidden).reshape(height, width, channels)
    early_terms, windows = tap_terms(flags, image, sides, early)
    pooled, block = at_cells(
        terms, w_key, w_value, standard, inverse, early_terms, windows
    )
    block, got = lax.optimization_barrier((block, got))
    blocks = lax.all_to_all(block, BOTH, 0, 0, tiled=True)
    rows = jnp.repeat(pooled, POOL, axis=0).reshape(2, width, channels)
    up = jnp.concatenate([pooled[0:1], pooled[4:5]], axis=0)
    down = jnp.concatenate([pooled[3:4], pooled[7:8]], axis=0)
    top, bottom = from_both_sides(
        (early[0] + rows[0]).astype(BF), (early[-1] + rows[1]).astype(BF), "row"
    )
    first = (early[:, 0] + jnp.repeat(up, POOL, axis=0)).astype(BF)
    last = (early[:, -1] + jnp.repeat(down, POOL, axis=0)).astype(BF)
    over = jnp.where(is_first, 0, top).astype(BF)
    under = jnp.where(is_last, 0, bottom).astype(BF)
    left, right = column_sides(
        jnp.concatenate([over[:1], first, under[:1]], axis=0),
        jnp.concatenate([over[-1:], last, under[-1:]], axis=0),
    )
    grad_image = unmix(flags, early, pooled, (top, bottom, left, right), conv_taps)
    placed, conv = pieces(flags, got, blocks, near, far)
    placed = lax.all_to_all(
        placed, BOTH, 0, 0, tiled=True, axis_index_groups=PLACE_GROUPS
    )
    grad_weights = jnp.transpose(placed.reshape(2, 192, half), (0, 2, 1)).reshape(channels, 192)
    grad_conv = jnp.concatenate([conv[:, 24:72], conv[:1, 72:120]], axis=0)
    return (grad_image, grad_weights.astype(F32), grad_conv)


def solution(mesh):
    return jax.shard_map(
        block_gradients,
        mesh=mesh,
        in_specs=(P("row", "col", None), P(), P(), P(), P(), P(), P("row", "col", None)),
        out_specs=(P("row", "col", None), P(None, "col"), P(None, "col")),
        check_vma=False,
    )
```

```python
import jax
import jax.numpy as jnp
from jax import lax
from jax.experimental import pallas as pl
from jax.experimental.pallas import tpu as pltpu
from jax.sharding import PartitionSpec as P

HD = 64
POOL = 8
EPSILON = 1e-05
BF = jnp.bfloat16
F32 = jnp.float32
LANES = 128
WIDE = 768

FINAL = (0, 1, 2, 3, 12, 13, 14, 15)
PARTNER = (5, 4, 7, 6, 9, 8, 11, 10)
SLICE_AT = tuple((FINAL.index(j) if j in FINAL else PARTNER.index(j)) for j in range(16))
PAIRS = [(j, j ^ 1) for j in range(16)]
OTHER_PAIRS = [(j, (j + (1 if j % 2 else -1)) % 16) for j in range(16)]
BOTH = ("row", "col")


def holder(piece, core):
    return FINAL[piece] if FINAL[piece] % 2 == core else PARTNER[piece]


SUM_GROUPS = [[q * 16 + holder(s, c) for s in range(8) for q in range(8)] for c in range(2)]
PLACE_GROUPS = [[q * 16 + holder(s, c) for c in range(2) for q in range(8)] for s in range(8)]


def from_both_sides(first, last, axis):
    count = lax.axis_size(axis)
    before = lax.ppermute(last, axis, [(i, (i + 1) % count) for i in range(count)])
    after = lax.ppermute(first, axis, [((i + 1) % count, i) for i in range(count)])
    return before, after


def column_sides(first, last):
    odd = lax.axis_index("col") % 2 == 1
    near = lax.ppermute(jnp.where(odd, first, last), "col", PAIRS)
    far = lax.ppermute(jnp.where(odd, last, first), "col", OTHER_PAIRS)
    return jnp.where(odd, near, far), jnp.where(odd, far, near)


def edges_of(tile, is_first, is_last):
    top, bottom = from_both_sides(tile[0], tile[-1], "row")
    up = jnp.where(is_first, 0, top).astype(BF)
    down = jnp.where(is_last, 0, bottom).astype(BF)
    first = jnp.concatenate([up[:1], tile[:, 0], down[:1]], axis=0)
    last = jnp.concatenate([up[-1:], tile[:, -1], down[-1:]], axis=0)
    left, right = column_sides(first, last)
    return top, bottom, left, right


def dot(left, right, dims):
    return lax.dot_general(left, right, ((dims[0], dims[1]), ((), ())), preferred_element_type=F32)


def contract_first(left, right):
    return dot(left, right, ((0,), (0,)))


def contract_last(left, right):
    return dot(left, right, ((1,), (1,)))


def put_sides(padded, flags, top, bottom, left, right):
    padded[0, 8:40, :] = top[...].astype(F32) * flags[0].astype(F32)
    padded[17, 8:40, :] = bottom[...].astype(F32) * flags[1].astype(F32)
    first = left[...].astype(F32) * flags[2].astype(F32)
    last = right[...].astype(F32) * flags[3].astype(F32)
    for row in range(18):
        padded[row, 7:8, :] = first[row : row + 1]
        padded[row, 40:41, :] = last[row : row + 1]


def windows_of(padded, at):
    kept = {}

    def window(row, shift):
        if (row, shift) not in kept:
            kept[row, shift] = padded[row, 7 + shift : 39 + shift, at]
        return kept[row, shift]

    return window


def mix_kernel(
    flags, image, top, bottom, left, right, taps, hidden, standard, inverse, normed, padded, pools
):
    step = pl.program_id(0)
    put_sides(padded, flags, top, bottom, left, right)
    padded[1:17, 8:40, :] = image[...].astype(F32)
    per = WIDE // LANES
    for part in range(per):
        at = slice(part * LANES, (part + 1) * LANES)
        weights = taps[:, at]
        window = windows_of(padded, at)
        for cell_row in range(2):
            column = jnp.zeros((32, LANES), F32)
            for row in range(cell_row * POOL, (cell_row + 1) * POOL):
                total = window(row + 1, 1)
                for a in range(3):
                    for b in range(3):
                        tap = 3 * a + b
                        total = total + weights[tap : tap + 1] * window(row + a, b)
                rounded = total.astype(BF)
                hidden[row * 32 : (row + 1) * 32, at] = rounded
                column = column + rounded.astype(F32)
            for cell in range(4):
                one = jnp.sum(column[cell * POOL : (cell + 1) * POOL], axis=0, keepdims=True)
                place = 4 * cell_row + cell
                pools[step * per + part, place : place + 1, :] = one * (1.0 / (POOL * POOL))

    @pl.when(step == pl.num_programs(0) - 1)
    def _():
        blocks = pools.shape[0]
        scale = 1.0 / (blocks * LANES)
        pooled = [pools[i] for i in range(blocks)]
        centre = sum(jnp.sum(x, axis=1, keepdims=True) for x in pooled) * scale
        moved = [x - centre for x in pooled]
        spread = sum(jnp.sum(x * x, axis=1, keepdims=True) for x in moved) * scale
        factor = lax.rsqrt(spread + EPSILON)
        inverse[...] = jnp.broadcast_to(factor, inverse.shape)
        for i in range(blocks):
            at = slice(i * LANES, (i + 1) * LANES)
            own = moved[i] * factor
            standard[:, at] = own
            normed[:, :, at] = jnp.broadcast_to(own.astype(BF)[None], (16, 8, LANES))


def side_specs():
    return [
        pl.BlockSpec((32, WIDE), lambda i: (0, i)),
        pl.BlockSpec((32, WIDE), lambda i: (0, i)),
        pl.BlockSpec((18, WIDE), lambda i: (0, i)),
        pl.BlockSpec((18, WIDE), lambda i: (0, i)),
    ]


SCALARS = pl.BlockSpec(memory_space=pltpu.SMEM)


def mix(flags, image, sides, taps):
    height, width, channels = image.shape
    return pl.pallas_call(
        mix_kernel,
        grid=(channels // WIDE,),
        in_specs=[
            SCALARS,
            pl.BlockSpec((height, width, WIDE), lambda i: (0, 0, i)),
            *side_specs(),
            pl.BlockSpec((9, WIDE), lambda i: (0, i)),
        ],
        out_specs=[
            pl.BlockSpec((height * width, WIDE), lambda i: (0, i)),
            pl.BlockSpec((8, channels), lambda i: (0, 0)),
            pl.BlockSpec((8, LANES), lambda i: (0, 0)),
            pl.BlockSpec((16, 8, channels), lambda i: (0, 0, 0)),
        ],
        out_shape=[
            jax.ShapeDtypeStruct((height * width, channels), BF),
            jax.ShapeDtypeStruct((8, channels), F32),
            jax.ShapeDtypeStruct((8, LANES), F32),
            jax.ShapeDtypeStruct((16, 8, channels), BF),
        ],
        scratch_shapes=[
            pltpu.VMEM((18, 48, WIDE), F32),
            pltpu.VMEM((channels // LANES, 8, LANES), F32),
        ],
        compiler_params=pltpu.CompilerParams(vmem_limit_bytes=16 << 20),
        cost_estimate=pl.CostEstimate(flops=8_000_000, bytes_accessed=2_000_000, transcendentals=0),
        name="mix",
    )(flags, image, *sides, taps)


def attend_kernel(query, dout, cells, w_key, w_value, attended, grad_query, sums):
    for pair in range(query.shape[1] // LANES):
        at = pl.ds(pair * LANES, LANES)
        attend_pair(
            query.at[:, at],
            dout.at[:, at],
            cells,
            w_key.at[:, at],
            w_value.at[:, at],
            attended.at[at],
            grad_query.at[at],
            sums.at[:, :, :, at],
        )


def attend_pair(query, dout, cells, w_key, w_value, attended, grad_query, sums):
    low = lax.broadcasted_iota(jnp.int32, (128, LANES), 1) < HD
    all_cells = cells[...]
    zero = jnp.zeros((128, LANES), BF)

    def two_heads(weight):
        both = jnp.dot(all_cells, weight[...], preferred_element_type=F32).astype(BF)
        return jnp.concatenate([jnp.where(low, both, zero), jnp.where(low, zero, both)], axis=0)

    keys = two_heads(w_key) * jnp.asarray(HD**-0.5, BF)
    values = two_heads(w_value)
    q, d = query[...], dout[...]
    expons = jnp.exp(contract_last(keys, q))
    grads = contract_last(values, d)
    probs, scores = [], []
    for head in range(2):
        own = expons[head * 128 : (head + 1) * 128]
        prob = own * (1.0 / jnp.sum(own, axis=0, keepdims=True))
        grad = grads[head * 128 : (head + 1) * 128]
        delta = jnp.sum(prob * grad, axis=0, keepdims=True)
        probs.append(prob.astype(BF))
        scores.append((prob * (grad - delta)).astype(BF))
    weights = jnp.concatenate(probs, axis=0)
    grad_scores = jnp.concatenate(scores, axis=0)
    attended[...] = contract_first(values, weights).astype(BF)
    grad_query[...] = contract_first(keys, grad_scores).astype(BF)
    grad_keys = jnp.dot(grad_scores, q, preferred_element_type=F32)
    grad_values = jnp.dot(weights, d, preferred_element_type=F32)
    grad_keys = jnp.where(low, grad_keys[:128], grad_keys[128:]) * (HD**-0.5)
    grad_values = jnp.where(low, grad_values[:128], grad_values[128:])
    sums[:, 0] = grad_keys.astype(BF).reshape(16, 8, LANES)
    sums[:, 1] = grad_values.astype(BF).reshape(16, 8, LANES)


def attend(query, dout, cells, w_key, w_value):
    tokens, channels = query.shape
    by_pair = pl.BlockSpec((tokens, 384), lambda i: (0, i))
    turned = pl.BlockSpec((384, tokens), lambda i: (i, 0))
    weight = pl.BlockSpec((channels, 384), lambda i: (0, i))
    return pl.pallas_call(
        attend_kernel,
        grid=(channels // 384,),
        in_specs=[
            by_pair,
            by_pair,
            pl.BlockSpec((128, channels), lambda i: (0, 0)),
            weight,
            weight,
        ],
        out_specs=[turned, turned, pl.BlockSpec((16, 2, 8, 384), lambda i: (0, 0, 0, i))],
        out_shape=[
            jax.ShapeDtypeStruct((channels, tokens), BF),
            jax.ShapeDtypeStruct((channels, tokens), BF),
            jax.ShapeDtypeStruct((16, 2, 8, channels), BF),
        ],
        cost_estimate=pl.CostEstimate(
            flops=3_000_000_000, bytes_accessed=6_000_000, transcendentals=800_000
        ),
        name="attend",
    )(query, dout, cells, w_key, w_value)


def chip_kernel(own_query, their_query, own_out, their_out, chip):
    chip[0] = (own_query[...].astype(F32) + their_query[...].astype(F32)).astype(BF)
    chip[1] = (own_out[...].astype(F32) + their_out[...].astype(F32)).astype(BF)


def chip_sums(own, theirs):
    rows, half = own[0].shape
    block = pl.BlockSpec((rows // 2, half), lambda i: (i, 0))
    return pl.pallas_call(
        chip_kernel,
        grid=(2,),
        in_specs=[block] * 4,
        out_specs=pl.BlockSpec((2, rows // 2, half), lambda i: (0, i, 0)),
        out_shape=jax.ShapeDtypeStruct((2, rows, half), BF),
        compiler_params=pltpu.CompilerParams(vmem_limit_bytes=16 << 20),
        cost_estimate=pl.CostEstimate(flops=1_200_000, bytes_accessed=3_500_000, transcendentals=0),
        name="chip_sums",
    )(own[0], theirs[0], own[1], theirs[1])


def taps_kernel(flags, image, top, bottom, left, right, early, terms, windows, padded, lines):
    put_sides(padded, flags, top, bottom, left, right)
    padded[1:17, 8:40, :] = image[...].astype(F32)
    for part in range(WIDE // LANES):
        at = slice(part * LANES, (part + 1) * LANES)
        window = windows_of(padded, at)
        totals = [jnp.zeros((8, LANES), F32) for _ in range(9)]
        for row in range(16):
            grad = early[row, :, at]
            for a in range(3):
                for b in range(3):
                    term = grad * window(row + a, b)
                    totals[3 * a + b] = totals[3 * a + b] + (
                        (term[:8] + term[8:16]) + (term[16:24] + term[24:])
                    )
        for tap in range(9):
            terms[tap : tap + 1, at] = jnp.sum(totals[tap], axis=0, keepdims=True)
    for cell_row in range(2):
        for a in range(3):
            start = cell_row * POOL + a
            line = padded[start]
            for row in range(start + 1, start + POOL):
                line = line + padded[row]
            lines[...] = line
            for b in range(3):
                for cell in range(4):
                    part = lines[7 + b + 8 * cell : 15 + b + 8 * cell, :]
                    place = 4 * cell_row + cell
                    windows[3 * a + b, place : place + 1, :] = jnp.sum(part, axis=0, keepdims=True)


def tap_terms(flags, image, sides, early):
    height, width, channels = image.shape
    block = pl.BlockSpec((height, width, WIDE), lambda i: (0, 0, i))
    return pl.pallas_call(
        taps_kernel,
        grid=(channels // WIDE,),
        in_specs=[SCALARS, block, *side_specs(), block],
        out_specs=[
            pl.BlockSpec((9, WIDE), lambda i: (0, i)),
            pl.BlockSpec((9, 8, WIDE), lambda i: (0, 0, i)),
        ],
        out_shape=[
            jax.ShapeDtypeStruct((9, channels), F32),
            jax.ShapeDtypeStruct((9, 8, channels), F32),
        ],
        scratch_shapes=[pltpu.VMEM((18, 48, WIDE), F32), pltpu.VMEM((48, WIDE), F32)],
        compiler_params=pltpu.CompilerParams(vmem_limit_bytes=16 << 20),
        cost_estimate=pl.CostEstimate(flops=8_000_000, bytes_accessed=3_000_000, transcendentals=0),
        name="tap_terms",
    )(flags, image, *sides, early)


def window_of(x, start):
    base = min(start // LANES * LANES, x.shape[1] - 2 * LANES)
    if start == base:
        return x[:, base : base + LANES]
    return pltpu.roll(x[:, base : base + 2 * LANES], base - start + 2 * LANES, 1)[:, :LANES]


def cells_kernel(terms, w_key, w_value, standard, inverse, early, windows, grad_pooled, blocks):
    received = jnp.sum(terms[...].astype(F32), axis=0)
    keys, values = received[0], received[1]
    grad = contract_last(keys.astype(BF), w_key[...]) + contract_last(values.astype(BF), w_value[...])
    own = standard[...]
    scale = 1.0 / own.shape[1]
    centre = jnp.sum(grad, axis=1, keepdims=True) * scale
    along = jnp.sum(grad * own, axis=1, keepdims=True) * scale
    pooled = (grad - centre - own * along) * (inverse[:, :1] * (1.0 / (POOL * POOL)))
    grad_pooled[...] = pooled
    conv = [
        early[t : t + 1, :] + jnp.sum(pooled * windows[t], axis=0, keepdims=True) for t in range(9)
    ]
    first, last = jnp.concatenate(conv[:8], axis=0), jnp.broadcast_to(conv[8], (8, own.shape[1]))
    lane = lax.broadcasted_iota(jnp.int32, (8, LANES), 1)
    both = jnp.concatenate([keys, values], axis=1)
    width = own.shape[1] // 16
    pieces = {}
    for j in range(16):
        part = PARTNER[SLICE_AT[j]] - 4
        taps = pltpu.roll(window_of(first, width * j), 24, 1)
        tail = pltpu.roll(window_of(last, width * j), 72, 1)
        rest = jnp.where(lane < 72, taps, tail)
        for q in range(8):
            if (part, q) not in pieces:
                pieces[part, q] = window_of(both, 192 * part + 24 * q)
            blocks[16 * q + j] = jnp.where(lane < 24, pieces[part, q], rest).astype(BF)


def at_cells(terms, w_key, w_value, standard, inverse, early, windows):
    channels = standard.shape[1]
    return pl.pallas_call(
        cells_kernel,
        out_shape=[
            jax.ShapeDtypeStruct((8, channels), F32),
            jax.ShapeDtypeStruct((128, 8, LANES), BF),
        ],
        compiler_params=pltpu.CompilerParams(vmem_limit_bytes=16 << 20),
        cost_estimate=pl.CostEstimate(flops=30_000_000, bytes_accessed=3_500_000, transcendentals=0),
        name="at_cells",
    )(terms, w_key, w_value, standard, inverse, early, windows)


def sum_kernel(got, total):
    total[...] = jnp.sum(got[...].astype(F32), axis=0).astype(BF)


def summed(got):
    return pl.pallas_call(
        sum_kernel,
        out_shape=jax.ShapeDtypeStruct(got.shape[1:], BF),
        compiler_params=pltpu.CompilerParams(vmem_limit_bytes=16 << 20),
        cost_estimate=pl.CostEstimate(flops=600_000, bytes_accessed=1_200_000, transcendentals=0),
        name="summed",
    )(got)


def pieces_kernel(flags, own, blocks, near, far, placed, conv):
    piece = own[...]
    conv[...] = jnp.sum(blocks[...].astype(F32), axis=0)
    total = jnp.zeros((LANES, piece.shape[1]), F32)
    for i in range(8):
        row = jnp.bitwise_xor(flags[5], i)
        own = blocks[pl.ds(row * 16, 16)].reshape(128, LANES)
        total = total + contract_first(own, near[i] if i < 4 else far[i - 4])
    cell_piece = total[:24].astype(BF)
    odd = flags[4] == 1
    first = jnp.where(odd, cell_piece, piece)
    second = jnp.where(odd, piece, cell_piece)
    for q in range(8):
        placed[q] = first
        placed[8 + q] = second


def pieces(flags, piece, blocks, near, far):
    half = near.shape[2]
    vmem = pl.BlockSpec(memory_space=pltpu.VMEM)
    return pl.pallas_call(
        pieces_kernel,
        in_specs=[SCALARS, vmem, vmem, vmem, vmem],
        out_shape=[
            jax.ShapeDtypeStruct((16, 24, half), BF),
            jax.ShapeDtypeStruct((8, LANES), F32),
        ],
        compiler_params=pltpu.CompilerParams(vmem_limit_bytes=16 << 20),
        cost_estimate=pl.CostEstimate(flops=100_000_000, bytes_accessed=2_500_000, transcendentals=0),
        name="pieces",
    )(flags, piece, blocks, near, far)


def unmix_kernel(flags, early, pooled, top, bottom, left, right, taps, image, padded):
    put_sides(padded, flags, top, bottom, left, right)
    for row in range(16):
        for cell in range(4):
            place = 4 * (row // POOL) + cell
            at = slice(8 * cell, 8 * cell + 8)
            padded[row + 1, 8 + 8 * cell : 16 + 8 * cell, :] = (
                early[row, at, :] + pooled[place : place + 1, :]
            )
    for part in range(WIDE // LANES):
        at = slice(part * LANES, (part + 1) * LANES)
        weights = taps[:, at]
        window = windows_of(padded, at)
        for row in range(16):
            total = window(row + 1, 1)
            for a in range(3):
                for b in range(3):
                    tap = 3 * a + b
                    total = total + weights[tap : tap + 1] * window(row + 2 - a, 2 - b)
            image[row, :, at] = total.astype(BF)


def unmix(flags, early, pooled, sides, taps):
    height, width, channels = early.shape
    block = pl.BlockSpec((height, width, WIDE), lambda i: (0, 0, i))
    return pl.pallas_call(
        unmix_kernel,
        grid=(channels // WIDE,),
        in_specs=[
            SCALARS,
            block,
            pl.BlockSpec((8, WIDE), lambda i: (0, i)),
            *side_specs(),
            pl.BlockSpec((9, WIDE), lambda i: (0, i)),
        ],
        out_specs=block,
        out_shape=jax.ShapeDtypeStruct((height, width, channels), BF),
        scratch_shapes=[pltpu.VMEM((18, 48, WIDE), F32)],
        compiler_params=pltpu.CompilerParams(vmem_limit_bytes=16 << 20),
        cost_estimate=pl.CostEstimate(flops=8_000_000, bytes_accessed=3_000_000, transcendentals=0),
        name="unmix",
    )(flags, early, pooled, *sides, taps)


def block_gradients(image, conv_taps, w_query, w_key, w_value, w_out, grad_out):
    height, width, channels = image.shape
    half = channels // 2
    at_row, at_col = lax.axis_index("row"), lax.axis_index("col")
    core = at_col % 2
    is_first, is_last = at_row == 0, at_row == lax.axis_size("row") - 1
    turned = (core == 1) ^ ((at_col >= 4) & (at_col < 12))
    flags = jnp.stack(
        [
            ~is_first,
            ~is_last,
            at_col > 0,
            at_col < lax.axis_size("col") - 1,
            turned,
        ]
    ).astype(jnp.int32)
    flags = jnp.concatenate([flags, at_row[None].astype(jnp.int32)])
    flat_grad = grad_out.reshape(-1, channels)
    sides = edges_of(image, is_first, is_last)
    dout = contract_last(flat_grad, w_out).astype(BF)
    hidden, standard, inverse, normed = mix(flags, image, sides, conv_taps)
    cells = lax.all_to_all(normed, "col", 0, 0, tiled=True)
    cells = cells.reshape(-1, channels)
    query = jnp.dot(hidden, w_query, preferred_element_type=F32).astype(BF)
    near = lax.dynamic_slice_in_dim(cells, core * half, half, axis=1)[None]
    for step in range(3):
        far = lax.ppermute(near, "row", [(i, i ^ (1 << step)) for i in range(8)])
        if step < 2:
            near = jnp.concatenate([near, far], axis=0)
    attended, grad_query, sums = attend(query, dout, cells, w_key, w_value)
    terms = lax.all_to_all(sums, "col", 0, 0, tiled=True)

    def half_terms(which):
        h = lax.dynamic_slice_in_dim(hidden, which * half, half, axis=1)
        a = lax.dynamic_slice_in_dim(attended, which * half, half, axis=0)
        return (
            dot(grad_query, h, ((1,), (0,))).astype(BF),
            dot(flat_grad, a, ((0,), (1,))).astype(BF),
        )

    sent = half_terms(1 - core)
    theirs = [lax.ppermute(x, "col", PAIRS) for x in sent]
    own = lax.optimization_barrier(half_terms(core))
    chip = chip_sums(own, theirs)
    got = lax.all_to_all(
        chip.reshape(64, 24, half), BOTH, 0, 0, tiled=True, axis_index_groups=SUM_GROUPS
    )
    grad_hidden = dot(grad_query, w_query, ((0,), (1,)))
    early = (flat_grad.astype(F32) + grad_hidden).reshape(height, width, channels)
    early_terms, windows = tap_terms(flags, image, sides, early)
    pooled, block = at_cells(
        terms, w_key, w_value, standard, inverse, early_terms, windows
    )
    block, got = lax.optimization_barrier((block, got))
    blocks = lax.all_to_all(block, BOTH, 0, 0, tiled=True)
    rows = jnp.repeat(pooled, POOL, axis=0).reshape(2, width, channels)
    up = jnp.concatenate([pooled[0:1], pooled[4:5]], axis=0)
    down = jnp.concatenate([pooled[3:4], pooled[7:8]], axis=0)
    top, bottom = from_both_sides(
        (early[0] + rows[0]).astype(BF), (early[-1] + rows[1]).astype(BF), "row"
    )
    first = (early[:, 0] + jnp.repeat(up, POOL, axis=0)).astype(BF)
    last = (early[:, -1] + jnp.repeat(down, POOL, axis=0)).astype(BF)
    over = jnp.where(is_first, 0, top).astype(BF)
    under = jnp.where(is_last, 0, bottom).astype(BF)
    left, right = column_sides(
        jnp.concatenate([over[:1], first, under[:1]], axis=0),
        jnp.concatenate([over[-1:], last, under[-1:]], axis=0),
    )
    grad_image = unmix(flags, early, pooled, (top, bottom, left, right), conv_taps)
    piece = summed(got)
    placed, conv = pieces(flags, piece, blocks, near, far)
    placed = lax.all_to_all(
        placed, BOTH, 0, 0, tiled=True, axis_index_groups=PLACE_GROUPS
    )
    grad_weights = jnp.transpose(placed.reshape(2, 192, half), (0, 2, 1)).reshape(channels, 192)
    grad_conv = jnp.concatenate([conv[:, 24:72], conv[:1, 72:120]], axis=0)
    return (grad_image, grad_weights.astype(F32), grad_conv)


def solution(mesh):
    return jax.shard_map(
        block_gradients,
        mesh=mesh,
        in_specs=(P("row", "col", None), P(), P(), P(), P(), P(), P("row", "col", None)),
        out_specs=(P("row", "col", None), P(None, "col"), P(None, "col")),
        check_vma=False,
    )
```

```python
import jax
import jax.numpy as jnp
from jax import lax
from jax.experimental import pallas as pl
from jax.experimental.pallas import tpu as pltpu
from jax.sharding import PartitionSpec as P

HD = 64
POOL = 8
EPSILON = 1e-05
BF = jnp.bfloat16
F32 = jnp.float32
LANES = 128
WIDE = 384

FINAL = (0, 1, 2, 3, 12, 13, 14, 15)
PARTNER = (5, 4, 7, 6, 9, 8, 11, 10)
SLICE_AT = tuple((FINAL.index(j) if j in FINAL else PARTNER.index(j)) for j in range(16))
PAIRS = [(j, j ^ 1) for j in range(16)]
OTHER_PAIRS = [(j, (j + (1 if j % 2 else -1)) % 16) for j in range(16)]
BOTH = ("row", "col")


def holder(piece, core):
    return FINAL[piece] if FINAL[piece] % 2 == core else PARTNER[piece]


SUM_GROUPS = [[q * 16 + holder(s, c) for s in range(8) for q in range(8)] for c in range(2)]
PLACE_GROUPS = [[q * 16 + holder(s, c) for c in range(2) for q in range(8)] for s in range(8)]


def from_both_sides(first, last, axis):
    count = lax.axis_size(axis)
    before = lax.ppermute(last, axis, [(i, (i + 1) % count) for i in range(count)])
    after = lax.ppermute(first, axis, [((i + 1) % count, i) for i in range(count)])
    return before, after


def column_sides(first, last):
    odd = lax.axis_index("col") % 2 == 1
    near = lax.ppermute(jnp.where(odd, first, last), "col", PAIRS)
    far = lax.ppermute(jnp.where(odd, last, first), "col", OTHER_PAIRS)
    return jnp.where(odd, near, far), jnp.where(odd, far, near)


def edges_of(tile, is_first, is_last):
    top, bottom = from_both_sides(tile[0], tile[-1], "row")
    up = jnp.where(is_first, 0, top).astype(BF)
    down = jnp.where(is_last, 0, bottom).astype(BF)
    first = jnp.concatenate([up[:1], tile[:, 0], down[:1]], axis=0)
    last = jnp.concatenate([up[-1:], tile[:, -1], down[-1:]], axis=0)
    left, right = column_sides(first, last)
    return top, bottom, left, right


def dot(left, right, dims):
    return lax.dot_general(left, right, ((dims[0], dims[1]), ((), ())), preferred_element_type=F32)


def contract_first(left, right):
    return dot(left, right, ((0,), (0,)))


def contract_last(left, right):
    return dot(left, right, ((1,), (1,)))


def put_sides(padded, flags, top, bottom, left, right):
    padded[0, 8:40, :] = top[...].astype(F32) * flags[0].astype(F32)
    padded[17, 8:40, :] = bottom[...].astype(F32) * flags[1].astype(F32)
    first = left[...].astype(F32) * flags[2].astype(F32)
    last = right[...].astype(F32) * flags[3].astype(F32)
    for row in range(18):
        padded[row, 7:8, :] = first[row : row + 1]
        padded[row, 40:41, :] = last[row : row + 1]


def windows_of(padded, at):
    kept = {}

    def window(row, shift):
        if (row, shift) not in kept:
            kept[row, shift] = padded[row, 7 + shift : 39 + shift, at]
        return kept[row, shift]

    return window


def mix_kernel(
    flags, image, top, bottom, left, right, taps, hidden, standard, inverse, normed, padded, pools
):
    step = pl.program_id(0)
    put_sides(padded, flags, top, bottom, left, right)
    padded[1:17, 8:40, :] = image[...].astype(F32)
    per = WIDE // LANES
    for part in range(per):
        at = slice(part * LANES, (part + 1) * LANES)
        weights = taps[:, at]
        window = windows_of(padded, at)
        for cell_row in range(2):
            column = jnp.zeros((32, LANES), F32)
            for row in range(cell_row * POOL, (cell_row + 1) * POOL):
                total = window(row + 1, 1)
                for a in range(3):
                    for b in range(3):
                        tap = 3 * a + b
                        total = total + weights[tap : tap + 1] * window(row + a, b)
                rounded = total.astype(BF)
                hidden[row * 32 : (row + 1) * 32, at] = rounded
                column = column + rounded.astype(F32)
            for cell in range(4):
                one = jnp.sum(column[cell * POOL : (cell + 1) * POOL], axis=0, keepdims=True)
                place = 4 * cell_row + cell
                pools[step * per + part, place : place + 1, :] = one * (1.0 / (POOL * POOL))

    @pl.when(step == pl.num_programs(0) - 1)
    def _():
        blocks = pools.shape[0]
        scale = 1.0 / (blocks * LANES)
        pooled = [pools[i] for i in range(blocks)]
        centre = sum(jnp.sum(x, axis=1, keepdims=True) for x in pooled) * scale
        moved = [x - centre for x in pooled]
        spread = sum(jnp.sum(x * x, axis=1, keepdims=True) for x in moved) * scale
        factor = lax.rsqrt(spread + EPSILON)
        inverse[...] = jnp.broadcast_to(factor, inverse.shape)
        for i in range(blocks):
            at = slice(i * LANES, (i + 1) * LANES)
            own = moved[i] * factor
            standard[:, at] = own
            normed[:, :, at] = jnp.broadcast_to(own.astype(BF)[None], (16, 8, LANES))


def side_specs():
    return [
        pl.BlockSpec((32, WIDE), lambda i: (0, i)),
        pl.BlockSpec((32, WIDE), lambda i: (0, i)),
        pl.BlockSpec((18, WIDE), lambda i: (0, i)),
        pl.BlockSpec((18, WIDE), lambda i: (0, i)),
    ]


SCALARS = pl.BlockSpec(memory_space=pltpu.SMEM)


def mix(flags, image, sides, taps):
    height, width, channels = image.shape
    return pl.pallas_call(
        mix_kernel,
        grid=(channels // WIDE,),
        in_specs=[
            SCALARS,
            pl.BlockSpec((height, width, WIDE), lambda i: (0, 0, i)),
            *side_specs(),
            pl.BlockSpec((9, WIDE), lambda i: (0, i)),
        ],
        out_specs=[
            pl.BlockSpec((height * width, WIDE), lambda i: (0, i)),
            pl.BlockSpec((8, channels), lambda i: (0, 0)),
            pl.BlockSpec((8, LANES), lambda i: (0, 0)),
            pl.BlockSpec((16, 8, channels), lambda i: (0, 0, 0)),
        ],
        out_shape=[
            jax.ShapeDtypeStruct((height * width, channels), BF),
            jax.ShapeDtypeStruct((8, channels), F32),
            jax.ShapeDtypeStruct((8, LANES), F32),
            jax.ShapeDtypeStruct((16, 8, channels), BF),
        ],
        scratch_shapes=[
            pltpu.VMEM((18, 48, WIDE), F32),
            pltpu.VMEM((channels // LANES, 8, LANES), F32),
        ],
        compiler_params=pltpu.CompilerParams(vmem_limit_bytes=16 << 20),
        cost_estimate=pl.CostEstimate(flops=8_000_000, bytes_accessed=2_000_000, transcendentals=0),
        name="mix",
    )(flags, image, *sides, taps)


def attend_kernel(query, dout, cells, w_key, w_value, attended, grad_query, sums):
    for pair in range(query.shape[1] // LANES):
        at = pl.ds(pair * LANES, LANES)
        attend_pair(
            query.at[:, at],
            dout.at[:, at],
            cells,
            w_key.at[:, at],
            w_value.at[:, at],
            attended.at[at],
            grad_query.at[at],
            sums.at[:, :, :, at],
        )


def attend_pair(query, dout, cells, w_key, w_value, attended, grad_query, sums):
    low = lax.broadcasted_iota(jnp.int32, (128, LANES), 1) < HD
    all_cells = cells[...]
    zero = jnp.zeros((128, LANES), BF)

    def two_heads(weight):
        both = jnp.dot(all_cells, weight[...], preferred_element_type=F32).astype(BF)
        return jnp.concatenate([jnp.where(low, both, zero), jnp.where(low, zero, both)], axis=0)

    keys = two_heads(w_key) * jnp.asarray(HD**-0.5, BF)
    values = two_heads(w_value)
    q, d = query[...], dout[...]
    expons = jnp.exp(contract_last(keys, q))
    grads = contract_last(values, d)
    probs, scores = [], []
    for head in range(2):
        own = expons[head * 128 : (head + 1) * 128]
        prob = own * (1.0 / jnp.sum(own, axis=0, keepdims=True))
        grad = grads[head * 128 : (head + 1) * 128]
        delta = jnp.sum(prob * grad, axis=0, keepdims=True)
        probs.append(prob.astype(BF))
        scores.append((prob * (grad - delta)).astype(BF))
    weights = jnp.concatenate(probs, axis=0)
    grad_scores = jnp.concatenate(scores, axis=0)
    attended[...] = contract_first(values, weights).astype(BF)
    grad_query[...] = contract_first(keys, grad_scores).astype(BF)
    grad_keys = jnp.dot(grad_scores, q, preferred_element_type=F32)
    grad_values = jnp.dot(weights, d, preferred_element_type=F32)
    grad_keys = jnp.where(low, grad_keys[:128], grad_keys[128:]) * (HD**-0.5)
    grad_values = jnp.where(low, grad_values[:128], grad_values[128:])
    sums[:, 0] = grad_keys.astype(BF).reshape(16, 8, LANES)
    sums[:, 1] = grad_values.astype(BF).reshape(16, 8, LANES)


def attend(query, dout, cells, w_key, w_value):
    tokens, channels = query.shape
    by_pair = pl.BlockSpec((tokens, 256), lambda i: (0, i))
    turned = pl.BlockSpec((256, tokens), lambda i: (i, 0))
    weight = pl.BlockSpec((channels, 256), lambda i: (0, i))
    return pl.pallas_call(
        attend_kernel,
        grid=(channels // 256,),
        in_specs=[
            by_pair,
            by_pair,
            pl.BlockSpec((128, channels), lambda i: (0, 0)),
            weight,
            weight,
        ],
        out_specs=[turned, turned, pl.BlockSpec((16, 2, 8, 256), lambda i: (0, 0, 0, i))],
        out_shape=[
            jax.ShapeDtypeStruct((channels, tokens), BF),
            jax.ShapeDtypeStruct((channels, tokens), BF),
            jax.ShapeDtypeStruct((16, 2, 8, channels), BF),
        ],
        cost_estimate=pl.CostEstimate(
            flops=3_000_000_000, bytes_accessed=6_000_000, transcendentals=800_000
        ),
        name="attend",
    )(query, dout, cells, w_key, w_value)


def chip_kernel(own_query, their_query, own_out, their_out, chip):
    chip[0] = (own_query[...].astype(F32) + their_query[...].astype(F32)).astype(BF)
    chip[1] = (own_out[...].astype(F32) + their_out[...].astype(F32)).astype(BF)


def chip_sums(own, theirs):
    rows, half = own[0].shape
    block = pl.BlockSpec((rows // 2, half), lambda i: (i, 0))
    return pl.pallas_call(
        chip_kernel,
        grid=(2,),
        in_specs=[block] * 4,
        out_specs=pl.BlockSpec((2, rows // 2, half), lambda i: (0, i, 0)),
        out_shape=jax.ShapeDtypeStruct((2, rows, half), BF),
        compiler_params=pltpu.CompilerParams(vmem_limit_bytes=16 << 20),
        cost_estimate=pl.CostEstimate(flops=1_200_000, bytes_accessed=3_500_000, transcendentals=0),
        name="chip_sums",
    )(own[0], theirs[0], own[1], theirs[1])


def taps_kernel(flags, image, top, bottom, left, right, early, terms, windows, padded, lines):
    put_sides(padded, flags, top, bottom, left, right)
    padded[1:17, 8:40, :] = image[...].astype(F32)
    for part in range(WIDE // LANES):
        at = slice(part * LANES, (part + 1) * LANES)
        window = windows_of(padded, at)
        totals = [jnp.zeros((8, LANES), F32) for _ in range(9)]
        for row in range(16):
            grad = early[row, :, at]
            for a in range(3):
                for b in range(3):
                    term = grad * window(row + a, b)
                    totals[3 * a + b] = totals[3 * a + b] + (
                        (term[:8] + term[8:16]) + (term[16:24] + term[24:])
                    )
        for tap in range(9):
            terms[tap : tap + 1, at] = jnp.sum(totals[tap], axis=0, keepdims=True)
    for cell_row in range(2):
        for a in range(3):
            start = cell_row * POOL + a
            line = padded[start]
            for row in range(start + 1, start + POOL):
                line = line + padded[row]
            lines[...] = line
            for b in range(3):
                for cell in range(4):
                    part = lines[7 + b + 8 * cell : 15 + b + 8 * cell, :]
                    place = 4 * cell_row + cell
                    windows[3 * a + b, place : place + 1, :] = jnp.sum(part, axis=0, keepdims=True)


def tap_terms(flags, image, sides, early):
    height, width, channels = image.shape
    block = pl.BlockSpec((height, width, WIDE), lambda i: (0, 0, i))
    return pl.pallas_call(
        taps_kernel,
        grid=(channels // WIDE,),
        in_specs=[SCALARS, block, *side_specs(), block],
        out_specs=[
            pl.BlockSpec((9, WIDE), lambda i: (0, i)),
            pl.BlockSpec((9, 8, WIDE), lambda i: (0, 0, i)),
        ],
        out_shape=[
            jax.ShapeDtypeStruct((9, channels), F32),
            jax.ShapeDtypeStruct((9, 8, channels), F32),
        ],
        scratch_shapes=[pltpu.VMEM((18, 48, WIDE), F32), pltpu.VMEM((48, WIDE), F32)],
        compiler_params=pltpu.CompilerParams(vmem_limit_bytes=16 << 20),
        cost_estimate=pl.CostEstimate(flops=8_000_000, bytes_accessed=3_000_000, transcendentals=0),
        name="tap_terms",
    )(flags, image, *sides, early)


def window_of(x, start):
    base = min(start // LANES * LANES, x.shape[1] - 2 * LANES)
    if start == base:
        return x[:, base : base + LANES]
    return pltpu.roll(x[:, base : base + 2 * LANES], base - start + 2 * LANES, 1)[:, :LANES]


def cells_kernel(terms, w_key, w_value, standard, inverse, early, windows, grad_pooled, blocks):
    received = jnp.sum(terms[...].astype(F32), axis=0)
    keys, values = received[0], received[1]
    grad = contract_last(keys.astype(BF), w_key[...]) + contract_last(values.astype(BF), w_value[...])
    own = standard[...]
    scale = 1.0 / own.shape[1]
    centre = jnp.sum(grad, axis=1, keepdims=True) * scale
    along = jnp.sum(grad * own, axis=1, keepdims=True) * scale
    pooled = (grad - centre - own * along) * (inverse[:, :1] * (1.0 / (POOL * POOL)))
    grad_pooled[...] = pooled
    conv = [
        early[t : t + 1, :] + jnp.sum(pooled * windows[t], axis=0, keepdims=True) for t in range(9)
    ]
    first, last = jnp.concatenate(conv[:8], axis=0), jnp.broadcast_to(conv[8], (8, own.shape[1]))
    lane = lax.broadcasted_iota(jnp.int32, (8, LANES), 1)
    both = jnp.concatenate([keys, values], axis=1)
    width = own.shape[1] // 16
    pieces = {}
    for j in range(16):
        part = PARTNER[SLICE_AT[j]] - 4
        taps = pltpu.roll(window_of(first, width * j), 24, 1)
        tail = pltpu.roll(window_of(last, width * j), 72, 1)
        rest = jnp.where(lane < 72, taps, tail)
        for q in range(8):
            if (part, q) not in pieces:
                pieces[part, q] = window_of(both, 192 * part + 24 * q)
            blocks[16 * q + j] = jnp.where(lane < 24, pieces[part, q], rest).astype(BF)


def at_cells(terms, w_key, w_value, standard, inverse, early, windows):
    channels = standard.shape[1]
    return pl.pallas_call(
        cells_kernel,
        out_shape=[
            jax.ShapeDtypeStruct((8, channels), F32),
            jax.ShapeDtypeStruct((128, 8, LANES), BF),
        ],
        compiler_params=pltpu.CompilerParams(vmem_limit_bytes=16 << 20),
        cost_estimate=pl.CostEstimate(flops=30_000_000, bytes_accessed=3_500_000, transcendentals=0),
        name="at_cells",
    )(terms, w_key, w_value, standard, inverse, early, windows)


def sum_kernel(got, total):
    total[...] = jnp.sum(got[...].astype(F32), axis=0).astype(BF)


def summed(got):
    return pl.pallas_call(
        sum_kernel,
        out_shape=jax.ShapeDtypeStruct(got.shape[1:], BF),
        compiler_params=pltpu.CompilerParams(vmem_limit_bytes=16 << 20),
        cost_estimate=pl.CostEstimate(flops=600_000, bytes_accessed=1_200_000, transcendentals=0),
        name="summed",
    )(got)


def pieces_kernel(flags, own, blocks, near, far, placed, conv):
    piece = own[...]
    conv[...] = jnp.sum(blocks[...].astype(F32), axis=0)
    total = jnp.zeros((LANES, piece.shape[1]), F32)
    for i in range(8):
        row = jnp.bitwise_xor(flags[5], i)
        own = blocks[pl.ds(row * 16, 16)].reshape(128, LANES)
        total = total + contract_first(own, near[i] if i < 4 else far[i - 4])
    cell_piece = total[:24].astype(BF)
    odd = flags[4] == 1
    first = jnp.where(odd, cell_piece, piece)
    second = jnp.where(odd, piece, cell_piece)
    for q in range(8):
        placed[q] = first
        placed[8 + q] = second


def pieces(flags, piece, blocks, near, far):
    half = near.shape[2]
    vmem = pl.BlockSpec(memory_space=pltpu.VMEM)
    return pl.pallas_call(
        pieces_kernel,
        in_specs=[SCALARS, vmem, vmem, vmem, vmem],
        out_shape=[
            jax.ShapeDtypeStruct((16, 24, half), BF),
            jax.ShapeDtypeStruct((8, LANES), F32),
        ],
        compiler_params=pltpu.CompilerParams(vmem_limit_bytes=16 << 20),
        cost_estimate=pl.CostEstimate(flops=100_000_000, bytes_accessed=2_500_000, transcendentals=0),
        name="pieces",
    )(flags, piece, blocks, near, far)


def unmix_kernel(flags, early, pooled, top, bottom, left, right, taps, image, padded):
    put_sides(padded, flags, top, bottom, left, right)
    for row in range(16):
        for cell in range(4):
            place = 4 * (row // POOL) + cell
            at = slice(8 * cell, 8 * cell + 8)
            padded[row + 1, 8 + 8 * cell : 16 + 8 * cell, :] = (
                early[row, at, :] + pooled[place : place + 1, :]
            )
    for part in range(WIDE // LANES):
        at = slice(part * LANES, (part + 1) * LANES)
        weights = taps[:, at]
        window = windows_of(padded, at)
        for row in range(16):
            total = window(row + 1, 1)
            for a in range(3):
                for b in range(3):
                    tap = 3 * a + b
                    total = total + weights[tap : tap + 1] * window(row + 2 - a, 2 - b)
            image[row, :, at] = total.astype(BF)


def unmix(flags, early, pooled, sides, taps):
    height, width, channels = early.shape
    block = pl.BlockSpec((height, width, WIDE), lambda i: (0, 0, i))
    return pl.pallas_call(
        unmix_kernel,
        grid=(channels // WIDE,),
        in_specs=[
            SCALARS,
            block,
            pl.BlockSpec((8, WIDE), lambda i: (0, i)),
            *side_specs(),
            pl.BlockSpec((9, WIDE), lambda i: (0, i)),
        ],
        out_specs=block,
        out_shape=jax.ShapeDtypeStruct((height, width, channels), BF),
        scratch_shapes=[pltpu.VMEM((18, 48, WIDE), F32)],
        compiler_params=pltpu.CompilerParams(vmem_limit_bytes=16 << 20),
        cost_estimate=pl.CostEstimate(flops=8_000_000, bytes_accessed=3_000_000, transcendentals=0),
        name="unmix",
    )(flags, early, pooled, *sides, taps)


def block_gradients(image, conv_taps, w_query, w_key, w_value, w_out, grad_out):
    height, width, channels = image.shape
    half = channels // 2
    at_row, at_col = lax.axis_index("row"), lax.axis_index("col")
    core = at_col % 2
    is_first, is_last = at_row == 0, at_row == lax.axis_size("row") - 1
    turned = (core == 1) ^ ((at_col >= 4) & (at_col < 12))
    flags = jnp.stack(
        [
            ~is_first,
            ~is_last,
            at_col > 0,
            at_col < lax.axis_size("col") - 1,
            turned,
        ]
    ).astype(jnp.int32)
    flags = jnp.concatenate([flags, at_row[None].astype(jnp.int32)])
    flat_grad = grad_out.reshape(-1, channels)
    sides = edges_of(image, is_first, is_last)
    dout = contract_last(flat_grad, w_out).astype(BF)
    hidden, standard, inverse, normed = mix(flags, image, sides, conv_taps)
    cells = lax.all_to_all(normed, "col", 0, 0, tiled=True)
    cells = cells.reshape(-1, channels)
    query = jnp.dot(hidden, w_query, preferred_element_type=F32).astype(BF)
    near = lax.dynamic_slice_in_dim(cells, core * half, half, axis=1)[None]
    for step in range(3):
        far = lax.ppermute(near, "row", [(i, i ^ (1 << step)) for i in range(8)])
        if step < 2:
            near = jnp.concatenate([near, far], axis=0)
    attended, grad_query, sums = attend(query, dout, cells, w_key, w_value)
    terms = lax.all_to_all(sums, "col", 0, 0, tiled=True)

    def half_terms(which):
        h = lax.dynamic_slice_in_dim(hidden, which * half, half, axis=1)
        a = lax.dynamic_slice_in_dim(attended, which * half, half, axis=0)
        return (
            dot(grad_query, h, ((1,), (0,))).astype(BF),
            dot(flat_grad, a, ((0,), (1,))).astype(BF),
        )

    sent = half_terms(1 - core)
    theirs = [lax.ppermute(x, "col", PAIRS) for x in sent]
    own = lax.optimization_barrier(half_terms(core))
    chip = chip_sums(own, theirs)
    got = lax.all_to_all(
        chip.reshape(64, 24, half), BOTH, 0, 0, tiled=True, axis_index_groups=SUM_GROUPS
    )
    grad_hidden = dot(grad_query, w_query, ((0,), (1,)))
    early = (flat_grad.astype(F32) + grad_hidden).reshape(height, width, channels)
    early_terms, windows = tap_terms(flags, image, sides, early)
    pooled, block = at_cells(
        terms, w_key, w_value, standard, inverse, early_terms, windows
    )
    block, got = lax.optimization_barrier((block, got))
    blocks = lax.all_to_all(block, BOTH, 0, 0, tiled=True)
    rows = jnp.repeat(pooled, POOL, axis=0).reshape(2, width, channels)
    up = jnp.concatenate([pooled[0:1], pooled[4:5]], axis=0)
    down = jnp.concatenate([pooled[3:4], pooled[7:8]], axis=0)
    top, bottom = from_both_sides(
        (early[0] + rows[0]).astype(BF), (early[-1] + rows[1]).astype(BF), "row"
    )
    first = (early[:, 0] + jnp.repeat(up, POOL, axis=0)).astype(BF)
    last = (early[:, -1] + jnp.repeat(down, POOL, axis=0)).astype(BF)
    over = jnp.where(is_first, 0, top).astype(BF)
    under = jnp.where(is_last, 0, bottom).astype(BF)
    left, right = column_sides(
        jnp.concatenate([over[:1], first, under[:1]], axis=0),
        jnp.concatenate([over[-1:], last, under[-1:]], axis=0),
    )
    grad_image = unmix(flags, early, pooled, (top, bottom, left, right), conv_taps)
    piece = summed(got)
    placed, conv = pieces(flags, piece, blocks, near, far)
    placed = lax.all_to_all(
        placed, BOTH, 0, 0, tiled=True, axis_index_groups=PLACE_GROUPS
    )
    grad_weights = jnp.transpose(placed.reshape(2, 192, half), (0, 2, 1)).reshape(channels, 192)
    grad_conv = jnp.concatenate([conv[:, 24:72], conv[:1, 72:120]], axis=0)
    return (grad_image, grad_weights.astype(F32), grad_conv)


def solution(mesh):
    return jax.shard_map(
        block_gradients,
        mesh=mesh,
        in_specs=(P("row", "col", None), P(), P(), P(), P(), P(), P("row", "col", None)),
        out_specs=(P("row", "col", None), P(None, "col"), P(None, "col")),
        check_vma=False,
    )
```
